256 devices in a mesh: slab: 16 (over x, y), pencil: 16 (over z, core).
Axes of the slice: x: 4, y: 4, z: 8, core: 2. Of those that a mesh axis runs over, the one named last changes fastest.
Arguments:
- charges: bfloat16 [64, 131072], P(None, ('slab', 'pencil')), may hold values from -6 to 6
- cotangent: bfloat16 [64, 131072], P(None, ('slab', 'pencil')), may hold values from -6 to 6
- base_cell: int32 [3, 131072], P(None, ('slab', 'pencil')), may hold values from 0 to 63, as said below
- frac: float32 [3, 131072], P(None, ('slab', 'pencil')), may hold values from 0 to 1
- counts: int32 [256], P(('slab', 'pencil')), may hold values from 256 to 512, as said below
- filter_weights: float32 [32, 64], replicated, may hold values from -6 to 6
Outputs:
- potential: bfloat16 [64, 131072], P(None, ('slab', 'pencil'))
- charge_grad: bfloat16 [64, 131072], P(None, ('slab', 'pencil'))
- filter_grad: float32 [32, 64], replicated
The draws below stay inside these ranges and needn't reach their ends.
Inputs may be any that keep to these rules, and one draw needn't show every extreme that they name: `base_cell`: slots d * 512 to (d + 1) * 512 - 1 belong to device d = slab index * (pencil axis size) + pencil index; their first cell index lies in the slab index's run of 4 cells and their second in the pencil index's run of 4 cells; the third is any cell. A device's live atoms are its first counts slots; some device's count is 512.
All inputs are finite; a program needn't handle non-finite values.
Results may differ from the reference program's by a relative error of at most 0.013.
Values may be sent and summed in bfloat16 or wider, within the bound.
A program may use at most 128 MiB of HBM per device.

```python
import jax
import jax.numpy as jnp
from jax import lax

N = 64
C = 64
NB = 32
ATOMS_DEV = 512
ATOMS = 131072
N_SLAB = 16
N_PENCIL = 16


def draw_base_cell(key, part):
    total = ATOMS_DEV * N_SLAB * N_PENCIL
    key_x, key_y, key_z = jax.random.split(key, 3)
    slot_index = jnp.arange(total, dtype=jnp.int32)
    device = slot_index // ATOMS_DEV
    slab_row = device // N_PENCIL
    pencil_col = device % N_PENCIL
    span_x = N // N_SLAB
    span_y = N // N_PENCIL
    cell_x = slab_row * span_x + jax.random.randint(key_x, (total,), 0, span_x)
    cell_y = pencil_col * span_y + jax.random.randint(key_y, (total,), 0, span_y)
    cell_z = jax.random.randint(key_z, (total,), 0, N)
    return jnp.stack([cell_x, cell_y, cell_z]).astype(jnp.int32)


def draw_counts(key, part):
    devices_all = N_SLAB * N_PENCIL
    key_levels, key_full = jax.random.split(key, 2)
    levels = jax.random.randint(key_levels, (devices_all,), ATOMS_DEV // 2, ATOMS_DEV + 1)
    fullest = jax.random.randint(key_full, (), 0, devices_all)
    return jnp.where(jnp.arange(devices_all) == fullest, ATOMS_DEV, levels).astype(jnp.int32)


def block_scale(stream_key, extent, cuts, low, largest):
    gain = 1.0
    for dim, parts in cuts:
        draws = jax.random.uniform(jax.random.fold_in(jax.random.fold_in(stream_key, 6), dim), (parts,), jnp.float32, low / len(cuts), largest / len(cuts))
        gain = gain * jnp.repeat(jnp.exp(draws), extent[dim] // parts).reshape((-1,) + (1,) * (len(extent) - 1 - dim))
    return gain


def normal_values(key, shape, scale, reach, shards=(), kind=jnp.bfloat16):
    array = scale * jax.random.normal(key, shape, jnp.float32)
    if shards:
        array = array * block_scale(key, shape, shards, -0.22, 0.18)
    return jnp.clip(array, -reach, reach).astype(kind)


def setup_inputs(seed: int = 0) -> dict:
    splits = jax.random.split(jax.random.key(seed), 7)
    charges = normal_values(splits[0], (C, ATOMS), 1.0, 6.0, ((1, 256),))
    cotangent = normal_values(splits[1], (C, ATOMS), 1.0, 6.0, ((1, 256),))
    base_cell = draw_base_cell(jax.random.fold_in(splits[6], 71), 0)
    frac = jnp.clip(1.0 * jax.random.uniform(splits[3], (3, ATOMS), jnp.float32) ** block_scale(splits[3], (3, ATOMS), ((1, 256),), -0.2, 0.2), 0.0, 1.0)
    counts = draw_counts(jax.random.fold_in(splits[6], 71), 0)
    filter_weights = normal_values(splits[5], (NB, C), 1.0, 6.0, (), jnp.float32)
    return {"charges": charges, "cotangent": cotangent, "base_cell": base_cell, "frac": frac, "counts": counts, "filter_weights": filter_weights}


ENV_SCALE = 40.0
ENV_WIDTH = 16.0

def spline_weights(frac):
    remain = 1.0 - frac
    square = frac * frac
    cubed = square * frac
    weight_zero = remain * remain * remain / 6.0
    weight_one = (3.0 * cubed - 6.0 * square + 4.0) / 6.0
    weight_two = (-3.0 * cubed + 3.0 * square + 3.0 * frac + 1.0) / 6.0
    weight_three = cubed / 6.0
    return jnp.stack([weight_zero, weight_one, weight_two, weight_three], axis=1)

def frequencies(positions):
    return jnp.where(positions < N // 2, positions, positions - N).astype(jnp.float32)

def grid_shells():
    freq_all = frequencies(jnp.arange(N, dtype=jnp.int32))
    kappa_sq = freq_all[:, None, None] * freq_all[:, None, None] + freq_all[None, :, None] * freq_all[None, :, None] + freq_all[None, None, :] * freq_all[None, None, :]
    kappa = jnp.sqrt(kappa_sq)
    envelope = ENV_SCALE * ENV_WIDTH / (ENV_WIDTH + kappa_sq)
    spacing = N / (2.0 * NB)
    centers = (jnp.arange(NB, dtype=jnp.float32) + 0.5) * spacing
    shells = envelope[..., None] * jnp.exp(-jnp.square((kappa[..., None] - centers) / spacing))
    return shells.reshape(N * N * N, NB)

def to_half(spectrum):
    real_part = jnp.real(spectrum).astype(jnp.bfloat16)
    imag_part = jnp.imag(spectrum).astype(jnp.bfloat16)
    real_part, imag_part = lax.optimization_barrier((real_part, imag_part))
    return lax.complex(real_part.astype(jnp.float32), imag_part.astype(jnp.float32))

def reference(charges, cotangent, base_cell, frac, counts, filter_weights):
    charges = charges.T
    cotangent = cotangent.T
    total = charges.shape[0]
    positions = jnp.arange(total, dtype=jnp.int32)
    live = (positions % ATOMS_DEV < counts[positions // ATOMS_DEV]).astype(jnp.float32)
    weights = spline_weights(frac)
    offsets = jnp.arange(64, dtype=jnp.int32)
    along_x = jnp.repeat(weights[0], 16, axis=0)
    along_y = jnp.tile(jnp.repeat(weights[1], 4, axis=0), (4, 1))
    along_z = jnp.tile(weights[2], (16, 1))
    stencil = along_x * along_y * along_z * live[None, :]
    cell_x = (base_cell[0][None, :] + offsets[:, None] // 16) % N
    cell_y = (base_cell[1][None, :] + offsets[:, None] // 4 % 4) % N
    cell_z = (base_cell[2][None, :] + offsets[:, None] % 4) % N
    cell_ids = ((cell_x * N + cell_y) * N + cell_z).astype(jnp.int32)
    shells = grid_shells()

    def spread_grid(values):

        def add_point(number, totals):
            return totals.at[cell_ids[number]].add(stencil[number][:, None] * values.astype(jnp.float32))
        grid = lax.fori_loop(0, 64, add_point, jnp.zeros((N * N * N, values.shape[1]), jnp.float32))
        return grid.reshape(N, N, N, values.shape[1])

    def gather_grid(grid):
        flattened = grid.reshape(N * N * N, grid.shape[3])

        def take_point(number, totals):
            return totals + stencil[number][:, None] * flattened[cell_ids[number]].astype(jnp.float32)
        summed = lax.fori_loop(0, 64, take_point, jnp.zeros((total, grid.shape[3]), jnp.float32))
        return summed.astype(jnp.bfloat16)

    def spectrum(density):
        section_one = to_half(jnp.fft.fft(density, axis=2))
        section_two = to_half(jnp.fft.fft(section_one, axis=1))
        return jnp.fft.fft(section_two, axis=0)

    def cells(filtered):
        section_one = to_half(jnp.fft.ifft(filtered, axis=0))
        section_two = to_half(jnp.fft.ifft(section_one, axis=1))
        return jnp.real(jnp.fft.ifft(section_two, axis=2)).astype(jnp.bfloat16)
    group = 8
    groups = C // group
    charge_groups = charges.reshape(total, groups, group).transpose(1, 0, 2)
    cot_groups = cotangent.reshape(total, groups, group).transpose(1, 0, 2)
    weight_groups = filter_weights.reshape(NB, groups, group).transpose(1, 0, 2)

    def one_group(inputs):
        charge_part, cot_part, weight_part = inputs
        profile = jnp.dot(shells, weight_part, precision=lax.Precision.HIGHEST).reshape(N, N, N, group)
        spectrum_q = spectrum(spread_grid(charge_part))
        potential_part = gather_grid(cells(profile * spectrum_q))
        spectrum_g = spectrum(spread_grid(cot_part))
        grad_part = gather_grid(cells(profile * spectrum_g))
        correlation = jnp.real(spectrum_g) * jnp.real(spectrum_q) + jnp.imag(spectrum_g) * jnp.imag(spectrum_q)
        weight_grad = jnp.dot(shells.T, correlation.reshape(N * N * N, group), precision=lax.Precision.HIGHEST) / (N * N * N)
        return (potential_part, grad_part, weight_grad)
    potentials, grads, weight_grads = lax.map(one_group, (charge_groups, cot_groups, weight_groups))
    potential = potentials.transpose(1, 0, 2).reshape(total, C)
    charge_grad = grads.transpose(1, 0, 2).reshape(total, C)
    filter_grad = weight_grads.transpose(1, 0, 2).reshape(NB, C)
    return (potential.T, charge_grad.T, filter_grad)
```

```python
import jax
import jax.numpy as jnp
import numpy as np
from jax import lax
from jax.sharding import PartitionSpec as P

C = 64
NB = 32
ENV_SCALE = 40.0
ENV_WIDTH = 16.0


def wave_order(groups):
    count = 4 * groups
    rows = []
    for g in range(groups):
        rows += [2 * g, 2 * g + 1, count - 2 * g if g else count // 2, count - 1 - 2 * g]
    return np.array(rows)


def dft_table(waves, count, inverse):
    angles = (waves[:, None] * np.arange(count)[None, :] % count) * (2.0 * np.pi / count)
    cosines, sines = np.cos(angles), np.sin(angles)
    if inverse:
        return np.concatenate([cosines.T, -sines.T], axis=1) / count
    return np.concatenate([cosines, sines], axis=1)


def turned(values):
    return jnp.concatenate([values[..., C:], -values[..., :C]], axis=-1)


def transform(values, axis, table):
    table = jnp.asarray(table, jnp.bfloat16)
    doubled = jnp.concatenate([values, turned(values)], axis=axis)
    out = lax.dot_general(table, doubled, (((1,), (axis,)), ((), ())), preferred_element_type=jnp.float32)
    return jnp.moveaxis(out, 0, axis)


def spline_weights(frac):
    remain = 1.0 - frac
    square = frac * frac
    cubed = square * frac
    return [
        remain * remain * remain / 6.0,
        (3.0 * cubed - 6.0 * square + 4.0) / 6.0,
        (-3.0 * cubed + 3.0 * square + 3.0 * frac + 1.0) / 6.0,
        cubed / 6.0,
    ]


def placed(weights, first, length, wrap):
    cells = lax.broadcasted_iota(jnp.int32, (length, first.shape[0]), 0)
    gap = cells - first[None, :]
    if wrap:
        gap = jnp.where(gap < 0, gap + length, gap)
    out = jnp.zeros(gap.shape, jnp.float32)
    for j in range(4):
        out = jnp.where(gap == j, weights[j][None, :], out)
    return out


def passed_along(value, axis, steps):
    count = lax.axis_size(axis)
    return lax.ppermute(value, axis, [(s, (s + steps) % count) for s in range(count)])


def frequency(waves, count):
    return jnp.where(waves < count // 2, waves, waves - count).astype(jnp.float32)


def local_waves(index, count):
    l = jnp.arange(4, dtype=jnp.int32)
    out = jnp.where(l < 2, 2 * index + l, count - 2 * index - (l - 2))
    return jnp.where((l == 2) & (index == 0), count // 2, out)


def per_device(charges, cotangent, base_cell, frac, counts, filter_weights):
    groups = lax.axis_size("slab")
    n = 4 * groups
    si = lax.axis_index("slab")
    pi = lax.axis_index("pencil")
    slots = charges.shape[1]
    vals = jnp.concatenate([charges, cotangent], axis=0)
    live = (jnp.arange(slots, dtype=jnp.int32) < counts[0]).astype(jnp.float32)
    wx = placed(spline_weights(frac[0]), base_cell[0] - 4 * si, 7, False) * live[None, :]
    wy = placed(spline_weights(frac[1]), base_cell[1] - 4 * pi, 7, False)
    wz = placed(spline_weights(frac[2]), base_cell[2], n, True)
    stencil = (wx[:, None, None, :] * wy[None, :, None, :] * wz[None, None, :, :]).astype(jnp.bfloat16)
    stencil = stencil.reshape(49 * n, slots)
    density = lax.dot_general(stencil, vals, (((1,), (1,)), ((), ())), preferred_element_type=jnp.float32)
    density = density.reshape(7, 7, n, 2 * C)
    up = passed_along(density[:, 5:].astype(jnp.bfloat16), "pencil", 1).astype(jnp.float32)
    down = passed_along(density[:, :1].astype(jnp.bfloat16), "pencil", -1).astype(jnp.float32)
    density = density[:, 1:5].at[:, :2].add(up).at[:, 3:].add(down)
    up = passed_along(density[5:].astype(jnp.bfloat16), "slab", 1).astype(jnp.float32)
    down = passed_along(density[:1].astype(jnp.bfloat16), "slab", -1).astype(jnp.float32)
    density = density[1:5].at[:2].add(up).at[3:].add(down).astype(jnp.bfloat16)

    waves = wave_order(groups)
    ahead = dft_table(waves, n, False)
    behind = dft_table((-waves) % n, n, False)
    back = dft_table(waves, n, True)
    spec = transform(density, 2, ahead).astype(jnp.bfloat16)
    spec = lax.all_to_all(spec, "pencil", split_axis=2, concat_axis=1, tiled=True)
    spec = transform(spec, 1, ahead).astype(jnp.bfloat16)
    spec = lax.all_to_all(spec, "slab", split_axis=1, concat_axis=0, tiled=True)
    both = transform(spec, 0, np.concatenate([ahead, behind], axis=0))
    spec, mirror = both[:n], both[n:]

    ky, kz = local_waves(si, n), local_waves(pi, n)
    fx = frequency(jnp.asarray(waves, jnp.int32), n)
    fy, fz = frequency(ky, n), frequency(kz, n)
    kappa_sq = fx[:, None, None] ** 2 + fy[None, :, None] ** 2 + fz[None, None, :] ** 2
    kappa = jnp.sqrt(kappa_sq)
    spacing = n / (2.0 * NB)
    centers = (jnp.arange(NB, dtype=jnp.float32) + 0.5) * spacing
    envelope = ENV_SCALE * ENV_WIDTH / (ENV_WIDTH + kappa_sq)
    shells = envelope[..., None] * jnp.exp(-jnp.square((kappa[..., None] - centers) / spacing))
    shells = shells.reshape(n * 16, NB)
    profile = jnp.dot(shells, jnp.tile(filter_weights, (1, 2)), precision=lax.Precision.HIGHEST)
    profile = profile.reshape(n, 4, 4, 2 * C)

    def flipped(values, axis, index):
        a, b, c, d = [lax.index_in_dim(values, l, axis) for l in range(4)]
        first = index == 0
        return jnp.concatenate([jnp.where(first, a, c), d, jnp.where(first, c, a), b], axis=axis)

    mirror = flipped(flipped(mirror, 1, si), 2, pi)
    mirror = jnp.concatenate([mirror[..., C:], mirror[..., :C]], axis=-1)
    product = (spec * mirror).reshape(n * 16, 2 * C)
    partial = jnp.dot(shells.T, product[:, :C] + product[:, C:], precision=lax.Precision.HIGHEST)
    partial = partial * (0.5 / (n * n * n))
    part = lax.all_to_all(partial.reshape(groups, NB // groups, C), "slab", 0, 0, tiled=True).sum(axis=0)
    part = lax.all_gather(part, "pencil").sum(axis=0)
    grad = lax.all_gather(part, "slab").reshape(NB, C)

    field = (spec * profile).astype(jnp.bfloat16)
    field = transform(field, 0, back).astype(jnp.bfloat16)
    field = lax.all_to_all(field, "slab", split_axis=0, concat_axis=1, tiled=True)
    field = transform(field, 1, back).astype(jnp.bfloat16)
    field = lax.all_to_all(field, "pencil", split_axis=1, concat_axis=2, tiled=True)
    field = transform(field, 2, back).astype(jnp.bfloat16)
    low = passed_along(field[3:], "slab", 1)
    high = passed_along(field[:2], "slab", -1)
    field = jnp.concatenate([low, field, high], axis=0)
    low = passed_along(field[:, 3:], "pencil", 1)
    high = passed_along(field[:, :2], "pencil", -1)
    field = jnp.concatenate([low, field, high], axis=1).reshape(49 * n, 2 * C)
    out = lax.dot_general(field, stencil, (((0,), (0,)), ((), ())), preferred_element_type=jnp.float32)
    out = out.astype(jnp.bfloat16)
    return (out[:C], out[C:], grad)


def solution(mesh):
    spread = P(None, ("slab", "pencil"))
    return jax.shard_map(
        per_device,
        mesh=mesh,
        in_specs=(spread, spread, spread, spread, P(("slab", "pencil")), P()),
        out_specs=(spread, spread, P()),
        check_vma=False,
    )
```

```python
import functools

import jax
import jax.numpy as jnp
import numpy as np
from jax import lax
from jax.experimental import pallas as pl
from jax.experimental.pallas import tpu as pltpu
from jax.sharding import PartitionSpec as P

C = 64
L = 2 * C
NB = 32
ENV_SCALE = 40.0
ENV_WIDTH = 16.0
MESH = pl.DeviceIdType.MESH
F32 = jnp.float32
BF16 = jnp.bfloat16


def wave_order(groups):
    count = 4 * groups
    rows = []
    for g in range(groups):
        rows += [2 * g, 2 * g + 1, count - 2 * g if g else count // 2, count - 1 - 2 * g]
    return np.array(rows)


def tables(groups):
    count = 4 * groups
    waves = wave_order(groups)
    eye = np.eye(4)

    def parts(rows, inverse):
        angles = (rows[:, None] * np.arange(count)[None, :] % count) * (2.0 * np.pi / count)
        cosines, sines = np.cos(angles), np.sin(angles)
        return (cosines.T / count, -sines.T / count) if inverse else (cosines, sines)

    def joined(pair, pattern=None):
        size = 4 * count
        if pattern is not None:
            split = [t.reshape(groups, 4, groups, 4) for t in pair]
            pair = [np.einsum(pattern, t, eye).reshape(size, size) for t in split]
        return jnp.asarray(np.concatenate(pair, axis=1), BF16)

    ahead, back = parts(waves, False), parts(waves, True)
    mirror = parts((-waves) % count, False)
    z_ahead = joined(ahead, "glhm,yv->gylvhm")
    y_ahead = joined(ahead, "glhm,ab->glahmb")
    x_ahead = jnp.concatenate([joined(ahead), joined(mirror)], axis=0)
    x_back = joined(back)
    y_back = joined(back, "glhm,ab->glahmb")
    z_back = joined(back, "glhm,yv->yglhvm")
    return z_ahead, y_ahead, x_ahead, x_back, y_back, z_back


def spline_weights(frac):
    remain = 1.0 - frac
    square = frac * frac
    cubed = square * frac
    return [
        remain * remain * remain / 6.0,
        (3.0 * cubed - 6.0 * square + 4.0) / 6.0,
        (-3.0 * cubed + 3.0 * square + 3.0 * frac + 1.0) / 6.0,
        cubed / 6.0,
    ]


def placed(gap, weights):
    out = jnp.zeros(gap.shape, F32)
    for j in range(4):
        out = jnp.where(gap == j, weights[j], out)
    return out


def squared_wave(group, inner, count):
    wave = jnp.where(inner < 2, 2 * group + inner, count - 2 * group - inner + 2)
    wave = jnp.where((inner == 2) & (group == 0), count // 2, wave)
    wave = jnp.where(wave < count // 2, wave, wave - count)
    return wave * wave


def kernel(
    groups, count_ref, charges_ref, cot_ref, base_ref, frac_ref, weights_ref,
    za_ref, ya_ref, xa_ref, xb_ref, yb_ref, zb_ref,
    pot_ref, cg_ref, grad_ref,
    wx_ref, wy_ref, wz_ref, st_ref, vals_ref, den_ref, ys_ref, yu_ref, yd_ref, xs_ref, xu_ref, xd_ref,
    send_ref, recv_ref, line_ref, spec_ref, mirror_ref, prof_ref, shell_ref, corr_ref, field_ref, acc_ref,
    g1s_ref, g1r_ref, g2s_ref, g2r_ref, g3s_ref, g3r_ref,
    hs, hr, es, er, local_sem,
):
    G = groups
    N = 4 * G
    R = 4 * N
    si = lax.axis_index("slab")
    pi = lax.axis_index("pencil")
    where_is = {"slab": si, "pencil": pi}
    slots = charges_ref.shape[1]

    barrier = pltpu.get_barrier_semaphore()

    def greet(d, carry):
        pl.semaphore_signal(barrier, inc=1, device_id={"slab": lax.rem(si + d, G)}, device_id_type=MESH)
        pl.semaphore_signal(barrier, inc=1, device_id={"pencil": lax.rem(pi + d, G)}, device_id_type=MESH)
        return carry

    lax.fori_loop(1, G, greet, 0)

    def shift(i, src, dst, axis, step):
        peer = lax.rem(where_is[axis] + step + G, G)
        return pltpu.make_async_remote_copy(
            src_ref=src, dst_ref=dst, send_sem=hs.at[i], recv_sem=hr.at[i],
            device_id={axis: peer}, device_id_type=MESH,
        )

    def hop(phase, src_of, dst, axis, d, to_peer):
        me = where_is[axis]
        peer = lax.rem(me + d, G)
        landed = me if to_peer else lax.rem(me + G - d, G)
        return pltpu.make_async_remote_copy(
            src_ref=src_of(peer), dst_ref=dst.at[landed], send_sem=es.at[phase, d], recv_sem=er.at[phase, d],
            device_id={axis: peer}, device_id_type=MESH,
        )

    def exchange(phase, src_of, dst, axis):
        def start(d, carry):
            hop(phase, src_of, dst, axis, d, True).start()
            return carry

        lax.fori_loop(1, G, start, 0)

    def arrived(phase, src_of, dst, axis):
        def wait(d, carry):
            hop(phase, src_of, dst, axis, d, False).wait_recv()
            return carry

        lax.fori_loop(1, G, wait, 0)

    def drained(phase, src_of, dst, axis):
        def wait(d, carry):
            hop(phase, src_of, dst, axis, d, True).wait_send()
            return carry

        lax.fori_loop(1, G, wait, 0)

    lane = lax.broadcasted_iota(jnp.int32, (1, L), 1)
    sign = jnp.where(lane < C, 1.0, -1.0).astype(F32)

    def stage(table_ref, pieces):
        columns = []
        for piece in pieces:
            wide = piece.astype(F32)
            turned = (pltpu.roll(wide, C, 1) * sign).astype(BF16)
            columns.append(jnp.concatenate([piece.astype(BF16), turned], axis=0))
        out = jnp.dot(table_ref[...], jnp.concatenate(columns, axis=1), preferred_element_type=F32)
        return [out[:, i * L:(i + 1) * L] for i in range(len(pieces))]

    live = lax.broadcasted_iota(jnp.int32, (1, slots), 1) < count_ref[0]
    row = lax.broadcasted_iota(jnp.int32, (8, slots), 0)
    cell = jnp.where(row < 6, row + 1, jnp.where(row == 6, 0, -8))
    wx = placed(cell - (base_ref[0:1, :] - 4 * si), spline_weights(frac_ref[0:1, :]))
    wx_ref[...] = jnp.where(live, wx, 0.0)
    wy_ref[...] = placed(cell - (base_ref[1:2, :] - 4 * pi), spline_weights(frac_ref[1:2, :]))
    gap = lax.broadcasted_iota(jnp.int32, (N, slots), 0) - base_ref[2:3, :]
    wz_ref[...] = placed(jnp.where(gap < 0, gap + N, gap), spline_weights(frac_ref[2:3, :]))
    vals_ref[...] = jnp.concatenate([charges_ref[...], cot_ref[...]], axis=0).T

    def spread(x, first, last):
        along_x = wx_ref[pl.ds(x, 1), :]
        for y in range(first, last):
            st_ref[x, y] = (wz_ref[...] * (along_x * wy_ref[y:y + 1, :])).astype(BF16)
        left = st_ref[x, first:last].reshape((last - first) * N, slots)
        return jnp.dot(left, vals_ref[...], preferred_element_type=F32)

    def rim_block(x, carry):
        ys_ref[x] = spread(x, 4, 7).astype(BF16).reshape(3, N, L)
        return carry

    def own_block(x, carry):
        den_ref[x] = spread(x, 0, 4).reshape(4, N, L)
        return carry

    lax.fori_loop(0, 7, rim_block, 0)
    pl.semaphore_wait(barrier, 2 * (G - 1))
    y_rims = [
        shift(0, ys_ref.at[4:7, 0:2], yu_ref.at[4:7], "pencil", 1),
        shift(1, ys_ref.at[4:7, 2:3], yd_ref.at[4:7], "pencil", -1),
        shift(2, ys_ref.at[0:4, 0:2], yu_ref.at[0:4], "pencil", 1),
        shift(3, ys_ref.at[0:4, 2:3], yd_ref.at[0:4], "pencil", -1),
    ]
    for copy in y_rims:
        copy.start()
    lax.fori_loop(0, 7, own_block, 0)

    y_rims[0].wait_recv()
    y_rims[1].wait_recv()
    for x in range(4, 7):
        xs_ref[x - 4, 0:2] = (den_ref[x, 0:2] + yu_ref[x].astype(F32)).astype(BF16)
        xs_ref[x - 4, 2:3] = den_ref[x, 2:3].astype(BF16)
        xs_ref[x - 4, 3:4] = (den_ref[x, 3:4] + yd_ref[x].astype(F32)).astype(BF16)
    x_rims = [
        shift(4, xs_ref.at[0:2], xu_ref, "slab", 1),
        shift(5, xs_ref.at[2:3], xd_ref, "slab", -1),
    ]
    for copy in x_rims:
        copy.start()
    y_rims[2].wait_recv()
    y_rims[3].wait_recv()
    for x in range(4):
        den_ref[x, 0:2] += yu_ref[x].astype(F32)
        den_ref[x, 3:4] += yd_ref[x].astype(F32)
    x_rims[0].wait_recv()
    x_rims[1].wait_recv()
    for x in range(2):
        den_ref[x] += xu_ref[x].astype(F32)
    den_ref[3] += xd_ref[0].astype(F32)

    def both_ways(phase, axis):
        return lambda peer: send_ref.at[phase, peer], recv_ref.at[phase], axis

    def run_stage(phase, table_ref, pieces_of):
        for x in range(0, 4, 2):
            for i, out in enumerate(stage(table_ref, [pieces_of(x), pieces_of(x + 1)])):
                send_ref[phase, :, x + i] = out.astype(BF16).reshape(G, 16, L)

    def begin(phase, axis):
        me = where_is[axis]
        exchange(phase, *both_ways(phase, axis))
        pltpu.make_async_copy(send_ref.at[phase, me], recv_ref.at[phase, me], local_sem.at[phase]).start()

    def finish(phase, axis):
        me = where_is[axis]
        arrived(phase, *both_ways(phase, axis))
        pltpu.make_async_copy(send_ref.at[phase, me], recv_ref.at[phase, me], local_sem.at[phase]).wait()

    run_stage(0, za_ref, lambda x: den_ref[x].reshape(R, L))
    begin(0, "pencil")

    at = lax.broadcasted_iota(jnp.int32, (NB, 16 * N), 1)
    block = at // N
    along = at % N
    kappa_sq = (
        squared_wave(along // 4, along % 4, N)
        + squared_wave(si, block // 4, N)
        + squared_wave(pi, block % 4, N)
    ).astype(F32)
    spacing = N / (2.0 * NB)
    centers = (lax.broadcasted_iota(jnp.int32, (NB, 16 * N), 0).astype(F32) + 0.5) * spacing
    reach = (jnp.sqrt(kappa_sq) - centers) / spacing
    shell_ref[...] = ENV_SCALE * ENV_WIDTH / (ENV_WIDTH + kappa_sq) * jnp.exp(-(reach * reach))
    doubled = jnp.concatenate([weights_ref[...], weights_ref[...]], axis=1)
    prof_ref[...] = lax.dot_general(
        shell_ref[...], doubled, (((0,), (0,)), ((), ())),
        precision=lax.Precision.HIGHEST, preferred_element_type=F32,
    ).reshape(16, N, L)

    finish(0, "pencil")
    run_stage(1, ya_ref, lambda x: recv_ref[0, :, x].reshape(R, L))
    begin(1, "slab")
    finish(1, "slab")

    line_ref[...] = recv_ref[1].reshape(16 * N, L).astype(F32)
    for b in range(0, 16, 2):
        lines = [line_ref[pl.ds(b + i, N, stride=16), :] for i in range(2)]
        outs = stage(xa_ref, lines)
        for i in range(2):
            spec_ref[b + i] = outs[i][:N]
            mirror_ref[b + i] = outs[i][N:]
    for b in range(0, 16, 2):
        outs = stage(xb_ref, [spec_ref[b + i] * prof_ref[b + i] for i in range(2)])
        for i in range(2):
            line_ref[pl.ds(b + i, N, stride=16), :] = outs[i]
    send_ref[2] = line_ref[...].astype(BF16).reshape(G, 4, 16, L)
    begin(2, "slab")

    for b in range(16):
        j, l = b // 4, b % 4
        jm = jnp.where(si == 0, (4 - j) % 4, (j + 2) % 4)
        lm = jnp.where(pi == 0, (4 - l) % 4, (l + 2) % 4)
        opposite = mirror_ref[jm * 4 + lm]
        corr_ref[pl.ds(b * N, N), :] = spec_ref[b] * pltpu.roll(opposite, C, 1)
    partial = jnp.dot(
        shell_ref[...], corr_ref[...], precision=lax.Precision.HIGHEST, preferred_element_type=F32
    )
    partial = (partial + pltpu.roll(partial, C, 1)) * (0.5 / (N * N * N))
    rows = NB // G
    g1s_ref[...] = jnp.zeros_like(g1s_ref)
    for g in range(G):
        g1s_ref[g, 0:rows, :] = partial[g * rows:(g + 1) * rows]
    first = (lambda peer: g1s_ref.at[peer], g1r_ref, "slab")
    second = (lambda peer: g2s_ref, g2r_ref, "pencil")
    third = (lambda peer: g3s_ref, g3r_ref, "slab")
    exchange(4, *first)
    g1r_ref[pl.ds(si, 1)] = g1s_ref[pl.ds(si, 1)]

    finish(2, "slab")
    run_stage(3, yb_ref, lambda x: recv_ref[2, :, x].reshape(R, L))
    begin(3, "pencil")

    arrived(4, *first)
    total = jnp.sum(g1r_ref[...], axis=0)
    g2s_ref[...] = total
    exchange(5, *second)
    g2r_ref[pl.ds(pi, 1)] = total[None]

    finish(3, "pencil")
    for x in range(0, 4, 2):
        pieces = [recv_ref[3, :, x + i].reshape(R, L) for i in range(2)]
        for i, out in enumerate(stage(zb_ref, pieces)):
            field_ref[x + i, 0:4] = out.astype(BF16).reshape(4, N, L)
    halo = [
        shift(6, field_ref.at[0:2, 0:4], field_ref.at[4:6, 0:4], "slab", -1),
        shift(7, field_ref.at[3:4, 0:4], field_ref.at[6:7, 0:4], "slab", 1),
        shift(8, field_ref.at[0:4, 0:2], field_ref.at[0:4, 4:6], "pencil", -1),
        shift(9, field_ref.at[0:4, 3:4], field_ref.at[0:4, 6:7], "pencil", 1),
    ]
    for copy in halo:
        copy.start()

    arrived(5, *second)
    total = jnp.sum(g2r_ref[...], axis=0)
    g3s_ref[...] = total
    exchange(6, *third)
    g3r_ref[pl.ds(si, 1)] = total[None]

    def gathered(x0, x1, y0, y1):
        depth = (x1 - x0) * (y1 - y0) * N
        return lax.dot_general(
            field_ref[x0:x1, y0:y1].reshape(depth, L), st_ref[x0:x1, y0:y1].reshape(depth, slots),
            (((0,), (0,)), ((), ())), preferred_element_type=F32,
        )

    acc_ref[...] = gathered(0, 4, 0, 4)
    halo[0].wait_recv()
    halo[1].wait_recv()
    corner = [
        shift(10, field_ref.at[4:7, 0:2], field_ref.at[4:7, 4:6], "pencil", -1),
        shift(11, field_ref.at[4:7, 3:4], field_ref.at[4:7, 6:7], "pencil", 1),
    ]
    for copy in corner:
        copy.start()
    acc_ref[...] += gathered(4, 7, 0, 4)
    halo[2].wait_recv()
    halo[3].wait_recv()
    acc_ref[...] += gathered(0, 4, 4, 7)
    corner[0].wait_recv()
    corner[1].wait_recv()
    total = acc_ref[...] + gathered(4, 7, 4, 7)
    pot_ref[...] = total[:C].astype(BF16)
    cg_ref[...] = total[C:].astype(BF16)

    arrived(6, *third)
    for g in range(G):
        grad_ref[g * rows:(g + 1) * rows, :] = g3r_ref[g, 0:rows, 0:C]
    for copy in y_rims + x_rims + halo + corner:
        copy.wait_send()
    for phase, axis in enumerate(["pencil", "slab", "slab", "pencil"]):
        drained(phase, *both_ways(phase, axis))
    drained(4, *first)
    drained(5, *second)
    drained(6, *third)


def per_device(charges, cotangent, base_cell, frac, counts, filter_weights):
    G = lax.axis_size("slab")
    N = 4 * G
    slots = charges.shape[1]
    vmem = pl.BlockSpec(memory_space=pltpu.VMEM)
    smem = pl.BlockSpec(memory_space=pltpu.SMEM)
    scratch = [
        pltpu.VMEM((8, slots), F32),
        pltpu.VMEM((8, slots), F32),
        pltpu.VMEM((N, slots), F32),
        pltpu.VMEM((7, 7, N, slots), BF16),
        pltpu.VMEM((slots, L), BF16),
        pltpu.VMEM((7, 4, N, L), F32),
        pltpu.VMEM((7, 3, N, L), BF16),
        pltpu.VMEM((7, 2, N, L), BF16),
        pltpu.VMEM((7, 1, N, L), BF16),
        pltpu.VMEM((3, 4, N, L), BF16),
        pltpu.VMEM((2, 4, N, L), BF16),
        pltpu.VMEM((1, 4, N, L), BF16),
        pltpu.VMEM((4, G, 4, 16, L), BF16),
        pltpu.VMEM((4, G, 4, 16, L), BF16),
        pltpu.VMEM((16 * N, L), F32),
        pltpu.VMEM((16, N, L), F32),
        pltpu.VMEM((16, N, L), F32),
        pltpu.VMEM((16, N, L), F32),
        pltpu.VMEM((NB, 16 * N), F32),
        pltpu.VMEM((16 * N, L), F32),
        pltpu.VMEM((7, 7, N, L), BF16),
        pltpu.VMEM((L, slots), F32),
        pltpu.VMEM((G, 8, L), F32),
        pltpu.VMEM((G, 8, L), F32),
        pltpu.VMEM((8, L), F32),
        pltpu.VMEM((G, 8, L), F32),
        pltpu.VMEM((8, L), F32),
        pltpu.VMEM((G, 8, L), F32),
        pltpu.SemaphoreType.DMA((12,)),
        pltpu.SemaphoreType.DMA((12,)),
        pltpu.SemaphoreType.DMA((7, G)),
        pltpu.SemaphoreType.DMA((7, G)),
        pltpu.SemaphoreType.DMA((4,)),
    ]
    return pl.pallas_call(
        functools.partial(kernel, G),
        out_shape=(
            jax.ShapeDtypeStruct((C, slots), BF16),
            jax.ShapeDtypeStruct((C, slots), BF16),
            jax.ShapeDtypeStruct((NB, C), F32),
        ),
        in_specs=[smem] + [vmem] * 11,
        out_specs=(vmem, vmem, vmem),
        scratch_shapes=scratch,
        compiler_params=pltpu.CompilerParams(
            collective_id=0, has_side_effects=True, vmem_limit_bytes=48 * 1024 * 1024
        ),
    )(counts, charges, cotangent, base_cell, frac, filter_weights, *tables(G))


def solution(mesh):
    spread = P(None, ("slab", "pencil"))
    return jax.shard_map(
        per_device,
        mesh=mesh,
        in_specs=(spread, spread, spread, spread, P(("slab", "pencil")), P()),
        out_specs=(spread, spread, P()),
        check_vma=False,
    )
```

```python
import functools

import jax
import jax.numpy as jnp
import numpy as np
from jax import lax
from jax.experimental import pallas as pl
from jax.experimental.pallas import tpu as pltpu
from jax.sharding import PartitionSpec as P

C = 64
L = 2 * C
NB = 32
ENV_SCALE = 40.0
ENV_WIDTH = 16.0
MESH = pl.DeviceIdType.MESH
F32 = jnp.float32
BF16 = jnp.bfloat16


def wave_order(groups):
    count = 4 * groups
    rows = []
    for g in range(groups):
        rows += [2 * g, 2 * g + 1, count - 2 * g if g else count // 2, count - 1 - 2 * g]
    return np.array(rows)


def tables(groups):
    count = 4 * groups
    waves = wave_order(groups)
    eye = np.eye(4)

    def parts(rows, cells, inverse):
        angles = (rows[:, None] * cells[None, :] % count) * (2.0 * np.pi / count)
        cosines, sines = np.cos(angles), np.sin(angles)
        return (cosines.T / count, -sines.T / count) if inverse else (cosines, sines)

    def joined(pair, pattern=None, inner=eye):
        size = 4 * count
        if pattern is not None:
            split = [t.reshape(groups, 4, groups, 4) for t in pair]
            pair = [np.einsum(pattern, t, inner).reshape(size, size) for t in split]
        return np.concatenate(pair, axis=1)

    every = np.arange(count)
    wide = (4 * np.arange(groups)[:, None] + np.arange(7)[None, :]).reshape(-1)
    ahead, back = parts(waves, every, False), parts(waves, every, True)
    mirror = parts((-waves) % count, every, False)
    y_ahead = joined(ahead, "glhm,ab->glahmb")
    across = [np.eye(4)[[(a + 2) % 4 for a in range(4)]], np.eye(4)[[(4 - a) % 4 for a in range(4)]]]
    made = [
        joined(ahead, "glhm,yv->gylvhm"),
        joined(parts(waves, wide, False)),
        np.stack([np.concatenate([y_ahead, joined(mirror, "glhm,ab->glahmb", t)]) for t in across]),
        joined(back, "glhm,ab->glahmb"),
        joined(parts(waves, wide, True)),
        joined(back, "glhm,yv->yglhvm"),
    ]
    return [jnp.asarray(t, BF16) for t in made]


def spline_weights(frac):
    remain = 1.0 - frac
    square = frac * frac
    cubed = square * frac
    return [
        remain * remain * remain / 6.0,
        (3.0 * cubed - 6.0 * square + 4.0) / 6.0,
        (-3.0 * cubed + 3.0 * square + 3.0 * frac + 1.0) / 6.0,
        cubed / 6.0,
    ]


def placed(gap, weights):
    out = jnp.zeros(gap.shape, F32)
    for j in range(4):
        out = jnp.where(gap == j, weights[j], out)
    return out


def squared_wave(group, inner, count):
    wave = jnp.where(inner < 2, 2 * group + inner, count - 2 * group - inner + 2)
    wave = jnp.where((inner == 2) & (group == 0), count // 2, wave)
    wave = jnp.where(wave < count // 2, wave, wave - count)
    return wave * wave


def kernel(
    groups, count_ref, charges_hbm, cot_hbm, base_hbm, frac_hbm, weights_hbm,
    za_hbm, xa_hbm, ya_hbm, yb_hbm, xb_hbm, zb_hbm,
    pot_ref, cg_ref, grad_ref,
    base_ref, frac_ref, both_ref, weights_ref, za_ref, xa_ref, ya_ref, yb_ref, xb_ref, zb_ref, load_sem,
    par_ref, near_par_ref, near_ref, wx_ref, wy_ref, wz_ref, st_ref, sn_ref, vals_ref, den_ref,
    s0_ref, r0_ref, s1_ref, r1_ref, s2_ref, r2_ref, s3_ref, r3_ref,
    wide_ref, line_ref, spec_ref, mirror_ref, prof_ref, shell_ref, corr_ref, field_ref, acc_ref, part_ref, back_ref,
    g1s_ref, g1r_ref, g2s_ref, g2r_ref, g3s_ref, g3r_ref,
    hs, hr, es, er, local_sem,
):
    G = groups
    N = 4 * G
    R = 4 * N
    si = lax.axis_index("slab")
    pi = lax.axis_index("pencil")
    where_is = {"slab": si, "pencil": pi}
    slots = charges_hbm.shape[1]

    barrier = pltpu.get_barrier_semaphore()

    def greet(d, carry):
        pl.semaphore_signal(barrier, inc=1, device_id={"pencil": lax.rem(pi + d, G)}, device_id_type=MESH)
        pl.semaphore_signal(barrier, inc=1, device_id={"slab": lax.rem(si + d, G)}, device_id_type=MESH)
        return carry

    lax.fori_loop(1, G, greet, 0)

    pairs = [
        (base_hbm, base_ref), (frac_hbm, frac_ref), (charges_hbm, both_ref.at[0:C]), (cot_hbm, both_ref.at[C:L]),
        (za_hbm, za_ref), (weights_hbm, weights_ref), (xa_hbm, xa_ref), (ya_hbm, ya_ref),
        (yb_hbm, yb_ref), (xb_hbm, xb_ref), (zb_hbm, zb_ref),
    ]
    owed = {}
    for i, (src, dst) in enumerate(pairs):
        load = pltpu.make_async_copy(src, dst, load_sem.at[i])
        load.start()
        owed["load", i] = load.wait

    def settle(*keys):
        for key in keys:
            owed.pop(key)()

    def shift(i, src, dst, step):
        copy = pltpu.make_async_remote_copy(
            src_ref=src, dst_ref=dst, send_sem=hs.at[i], recv_sem=hr.at[i],
            device_id={"pencil": lax.rem(pi + step + G, G)}, device_id_type=MESH,
        )
        copy.start()
        owed["shift", i] = copy.wait_recv
        owed["sent", i] = copy.wait_send

    def exchange(phase, src_of, dst, axis):
        me = where_is[axis]

        def hop(d, landed):
            peer = lax.rem(me + d, G)
            return pltpu.make_async_remote_copy(
                src_ref=src_of(peer), dst_ref=dst.at[landed], send_sem=es.at[phase, d], recv_sem=er.at[phase, d],
                device_id={axis: peer}, device_id_type=MESH,
            )

        def start(d, carry):
            hop(d, me).start()
            return carry

        def arrive(d, carry):
            hop(d, lax.rem(me + G - d, G)).wait_recv()
            return carry

        def drain(d, carry):
            hop(d, me).wait_send()
            return carry

        lax.fori_loop(1, G, start, 0)
        owed["exchange", phase] = lambda: lax.fori_loop(1, G, arrive, 0)
        owed["gone", phase] = lambda: lax.fori_loop(1, G, drain, 0)

    def begin(phase, src, dst, axis):
        me = where_is[axis]
        exchange(phase, lambda peer: src.at[peer], dst, axis)
        own = pltpu.make_async_copy(src.at[me], dst.at[me], local_sem.at[phase])
        own.start()
        owed["own", phase] = own.wait

    def finish(phase):
        settle(("exchange", phase), ("own", phase))

    lane = lax.broadcasted_iota(jnp.int32, (1, L), 1)
    sign = jnp.where(lane < C, 1.0, -1.0).astype(F32)

    def stage(table, pieces):
        columns = []
        for piece in pieces:
            wide = piece.astype(F32)
            turned = (pltpu.roll(wide, C, 1) * sign).astype(BF16)
            columns.append(jnp.concatenate([piece.astype(BF16), turned], axis=0))
        out = jnp.dot(table, jnp.concatenate(columns, axis=1), preferred_element_type=F32)
        return [out[:, i * L:(i + 1) * L] for i in range(len(pieces))]

    settle(("load", 0), ("load", 1))
    live = lax.broadcasted_iota(jnp.int32, (1, slots), 1) < count_ref[0]
    par_ref[0:3, :] = frac_ref[...]
    par_ref[3:6, :] = base_ref[...].astype(F32)
    par_ref[6:7, :] = live.astype(F32)
    par_ref[7:8, :] = jnp.zeros((1, slots), F32)
    settle(("load", 2), ("load", 3))
    pl.semaphore_wait(barrier, 2 * (G - 1))
    shift(0, par_ref, near_par_ref, 1)
    shift(1, both_ref, near_ref, 1)

    def weigh(par, block, first_row):
        row = lax.broadcasted_iota(jnp.int32, (8, slots), 0).astype(F32)
        wx = placed(row - (par[3:4, :] - (4 * si).astype(F32)), spline_weights(par[0:1, :]))
        wx_ref[...] = wx * par[6:7, :]
        wy_ref[...] = placed(row + first_row - (par[4:5, :] - (4 * block).astype(F32)), spline_weights(par[1:2, :]))
        gap = lax.broadcasted_iota(jnp.int32, (N, slots), 0).astype(F32) - par[5:6, :]
        wz_ref[...] = placed(jnp.where(gap < 0, gap + N, gap), spline_weights(par[2:3, :]))

    def spread(stencil_ref, x, rows):
        along_x = wx_ref[pl.ds(x, 1), :]
        for y in range(rows):
            stencil_ref[x, y] = (wz_ref[...] * (along_x * wy_ref[y:y + 1, :])).astype(BF16)
        left = stencil_ref[x].reshape(rows * N, slots)
        return jnp.dot(left, vals_ref[...], preferred_element_type=F32)

    def own_plane(x, carry):
        den_ref[x] = spread(st_ref, x, 4)
        return carry

    def near_plane(x, carry):
        den_ref[x, 0:3 * N] += spread(sn_ref, x, 3)
        return carry

    weigh(par_ref, pi, 0.0)
    vals_ref[...] = both_ref[...].T
    lax.fori_loop(0, 7, own_plane, 0)
    settle(("load", 4), ("shift", 0), ("shift", 1))
    weigh(near_par_ref, lax.rem(pi + G - 1, G), 4.0)
    vals_ref[...] = near_ref[...].T
    lax.fori_loop(0, 7, near_plane, 0)
    for x in range(0, 7, 2):
        pieces = [den_ref[i] for i in range(x, min(x + 2, 7))]
        for i, out in enumerate(stage(za_ref[...], pieces)):
            s0_ref[:, x + i] = out.astype(BF16).reshape(G, 16, L)
    begin(0, s0_ref, r0_ref, "slab")

    settle(*[("load", i) for i in range(5, 11)])
    at = lax.broadcasted_iota(jnp.int32, (NB, 16 * N), 1)
    along = at // 4 % N
    kappa_sq = (
        squared_wave(pi, at // R, N) + squared_wave(along // 4, along % 4, N) + squared_wave(si, at % 4, N)
    ).astype(F32)
    spacing = N / (2.0 * NB)
    centers = (lax.broadcasted_iota(jnp.int32, (NB, 16 * N), 0).astype(F32) + 0.5) * spacing
    reach = (jnp.sqrt(kappa_sq) - centers) / spacing
    shell_ref[...] = ENV_SCALE * ENV_WIDTH / (ENV_WIDTH + kappa_sq) * jnp.exp(-(reach * reach))
    doubled = jnp.concatenate([weights_ref[...], weights_ref[...]], axis=1)
    prof_ref[...] = lax.dot_general(
        shell_ref[...], doubled, (((0,), (0,)), ((), ())),
        precision=lax.Precision.HIGHEST, preferred_element_type=F32,
    ).reshape(4, R, L)

    finish(0)
    wide_ref[...] = r0_ref[...].reshape(7 * 16 * G, L).astype(F32)
    for b in range(0, 16, 2):
        outs = stage(xa_ref[...], [wide_ref[pl.ds(b + i, 7 * G, stride=16), :] for i in range(2)])
        for i in range(2):
            line_ref[pl.ds(b + i, N, stride=16), :] = outs[i]
    s1_ref[...] = line_ref[...].astype(BF16).reshape(G, 4, 16, L)
    begin(1, s1_ref, r1_ref, "pencil")
    finish(1)

    flip = jnp.where(si == 0, 1, 0)
    for x in range(0, 4, 2):
        outs = stage(ya_ref[flip], [r1_ref[:, x + i].reshape(R, L) for i in range(2)])
        for i in range(2):
            spec_ref[x + i] = outs[i][:R]
            mirror_ref[x + i] = outs[i][R:]
        outs = stage(yb_ref[...], [spec_ref[x + i] * prof_ref[x + i] for i in range(2)])
        for i in range(2):
            s2_ref[:, x + i] = outs[i].astype(BF16).reshape(G, 16, L)
    begin(2, s2_ref, r2_ref, "pencil")

    for x in range(4):
        opposite = jnp.where(pi == 0, (4 - x) % 4, (x + 2) % 4)
        corr_ref[pl.ds(x * R, R), :] = spec_ref[x] * pltpu.roll(mirror_ref[opposite], C, 1)
    partial = jnp.dot(
        shell_ref[...], corr_ref[...], precision=lax.Precision.HIGHEST, preferred_element_type=F32
    )
    partial = (partial + pltpu.roll(partial, C, 1)) * (0.5 / (N * N * N))
    rows = NB // G
    g1s_ref[...] = jnp.zeros_like(g1s_ref)
    for g in range(G):
        g1s_ref[g, 0:rows, :] = partial[g * rows:(g + 1) * rows]
    exchange(4, lambda peer: g1s_ref.at[peer], g1r_ref, "pencil")
    g1r_ref[pl.ds(pi, 1)] = g1s_ref[pl.ds(pi, 1)]

    finish(2)
    line_ref[...] = r2_ref[...].reshape(16 * N, L).astype(F32)
    for b in range(0, 16, 2):
        outs = stage(xb_ref[...], [line_ref[pl.ds(b + i, N, stride=16), :] for i in range(2)])
        for i in range(2):
            wide_ref[pl.ds(b + i, 7 * G, stride=16), :] = outs[i]
    s3_ref[...] = wide_ref[...].astype(BF16).reshape(G, 7, 16, L)
    begin(3, s3_ref, r3_ref, "slab")

    settle(("exchange", 4))
    total = jnp.sum(g1r_ref[...], axis=0)
    g2s_ref[...] = total
    exchange(5, lambda peer: g2s_ref, g2r_ref, "slab")
    g2r_ref[pl.ds(si, 1)] = total[None]

    finish(3)
    for x in range(0, 7, 2):
        pieces = [r3_ref[:, i].reshape(R, L) for i in range(x, min(x + 2, 7))]
        for i, out in enumerate(stage(zb_ref[...], pieces)):
            field_ref[x + i] = out.astype(BF16)

    def gathered(stencil_ref, rows):
        depth = 7 * rows * N
        return lax.dot_general(
            field_ref[:, 0:rows * N].reshape(depth, L), stencil_ref[...].reshape(depth, slots),
            (((0,), (0,)), ((), ())), preferred_element_type=F32,
        )

    part_ref[...] = gathered(sn_ref, 3).astype(BF16)
    shift(2, part_ref, back_ref, -1)

    settle(("exchange", 5))
    total = jnp.sum(g2r_ref[...], axis=0)
    g3s_ref[...] = total
    exchange(6, lambda peer: g3s_ref, g3r_ref, "pencil")
    g3r_ref[pl.ds(pi, 1)] = total[None]

    acc_ref[...] = gathered(st_ref, 4)
    settle(("shift", 2))
    pot_ref[...] = (acc_ref[0:C] + back_ref[0:C].astype(F32)).astype(BF16)
    cg_ref[...] = (acc_ref[C:L] + back_ref[C:L].astype(F32)).astype(BF16)

    settle(("exchange", 6))
    for g in range(G):
        grad_ref[g * rows:(g + 1) * rows, :] = g3r_ref[g, 0:rows, 0:C]
    for wait in owed.values():
        wait()


def per_device(charges, cotangent, base_cell, frac, counts, filter_weights):
    G = lax.axis_size("slab")
    N = 4 * G
    slots = charges.shape[1]
    dft = tables(G)
    vmem = pl.BlockSpec(memory_space=pltpu.VMEM)
    smem = pl.BlockSpec(memory_space=pltpu.SMEM)
    hbm = pl.BlockSpec(memory_space=pltpu.HBM)
    wide = pltpu.VMEM((G, 7, 16, L), BF16)
    slim = pltpu.VMEM((G, 4, 16, L), BF16)
    tiles = pltpu.VMEM((G, 8, L), F32)
    tile = pltpu.VMEM((8, L), F32)
    scratch = [
        pltpu.VMEM((3, slots), jnp.int32),
        pltpu.VMEM((3, slots), F32),
        pltpu.VMEM((L, slots), BF16),
        pltpu.VMEM((NB, C), F32),
        *[pltpu.VMEM(t.shape, BF16) for t in dft],
        pltpu.SemaphoreType.DMA((11,)),
        pltpu.VMEM((8, slots), F32),
        pltpu.VMEM((8, slots), F32),
        pltpu.VMEM((L, slots), BF16),
        pltpu.VMEM((8, slots), F32),
        pltpu.VMEM((8, slots), F32),
        pltpu.VMEM((N, slots), F32),
        pltpu.VMEM((7, 4, N, slots), BF16),
        pltpu.VMEM((7, 3, N, slots), BF16),
        pltpu.VMEM((slots, L), BF16),
        pltpu.VMEM((7, 4 * N, L), F32),
        wide, wide, slim, slim, slim, slim, wide, wide,
        pltpu.VMEM((7 * 16 * G, L), F32),
        pltpu.VMEM((16 * N, L), F32),
        pltpu.VMEM((4, 4 * N, L), F32),
        pltpu.VMEM((4, 4 * N, L), F32),
        pltpu.VMEM((4, 4 * N, L), F32),
        pltpu.VMEM((NB, 16 * N), F32),
        pltpu.VMEM((16 * N, L), F32),
        pltpu.VMEM((7, 4 * N, L), BF16),
        pltpu.VMEM((L, slots), F32),
        pltpu.VMEM((L, slots), BF16),
        pltpu.VMEM((L, slots), BF16),
        tiles, tiles, tile, tiles, tile, tiles,
        pltpu.SemaphoreType.DMA((3,)),
        pltpu.SemaphoreType.DMA((3,)),
        pltpu.SemaphoreType.DMA((7, G)),
        pltpu.SemaphoreType.DMA((7, G)),
        pltpu.SemaphoreType.DMA((4,)),
    ]
    return pl.pallas_call(
        functools.partial(kernel, G),
        out_shape=(
            jax.ShapeDtypeStruct((C, slots), BF16),
            jax.ShapeDtypeStruct((C, slots), BF16),
            jax.ShapeDtypeStruct((NB, C), F32),
        ),
        in_specs=[smem] + [hbm] * 11,
        out_specs=(vmem, vmem, vmem),
        scratch_shapes=scratch,
        compiler_params=pltpu.CompilerParams(
            collective_id=0, has_side_effects=True, vmem_limit_bytes=67043328
        ),
    )(counts, charges, cotangent, base_cell, frac, filter_weights, *dft)


def solution(mesh):
    spread = P(None, ("slab", "pencil"))
    return jax.shard_map(
        per_device,
        mesh=mesh,
        in_specs=(spread, spread, spread, spread, P(("slab", "pencil")), P()),
        out_specs=(spread, spread, P()),
        check_vma=False,
    )
```

```python
import functools

import jax
import jax.numpy as jnp
import numpy as np
from jax import lax
from jax.experimental import pallas as pl
from jax.experimental.pallas import tpu as pltpu
from jax.sharding import PartitionSpec as P

C = 64
L = 2 * C
NB = 32
ENV_SCALE = 40.0
ENV_WIDTH = 16.0
MESH = pl.DeviceIdType.MESH
F32 = jnp.float32
BF16 = jnp.bfloat16


def wave_order(groups):
    count = 4 * groups
    rows = []
    for g in range(groups):
        rows += [2 * g, 2 * g + 1, count - 2 * g if g else count // 2, count - 1 - 2 * g]
    return np.array(rows)


def tables(groups):
    count = 4 * groups
    waves = wave_order(groups)
    eye = np.eye(4)

    def parts(rows, cells, inverse):
        angles = (rows[:, None] * cells[None, :] % count) * (2.0 * np.pi / count)
        cosines, sines = np.cos(angles), np.sin(angles)
        return (cosines.T / count, -sines.T / count) if inverse else (cosines, sines)

    def joined(pair, pattern=None, inner=eye):
        size = 4 * count
        if pattern is not None:
            split = [t.reshape(groups, 4, groups, 4) for t in pair]
            pair = [np.einsum(pattern, t, inner).reshape(size, size) for t in split]
        return np.concatenate(pair, axis=1)

    every = np.arange(count)
    wide = (4 * np.arange(groups)[:, None] + np.arange(7)[None, :]).reshape(-1)
    ahead, back = parts(waves, every, False), parts(waves, every, True)
    mirror = parts((-waves) % count, every, False)
    y_ahead = joined(ahead, "glhm,ab->glahmb")
    across = [np.eye(4)[[(a + 2) % 4 for a in range(4)]], np.eye(4)[[(4 - a) % 4 for a in range(4)]]]
    made = [
        joined(ahead, "glhm,yv->gylvhm"),
        joined(parts(waves, wide, False)),
        np.stack([np.concatenate([y_ahead, joined(mirror, "glhm,ab->glahmb", t)]) for t in across]),
        joined(back, "glhm,ab->glahmb"),
        joined(parts(waves, wide, True)),
        joined(back, "glhm,yv->yglhvm"),
    ]
    return [jnp.asarray(t, BF16) for t in made]


def spline_weights(frac):
    remain = 1.0 - frac
    square = frac * frac
    cubed = square * frac
    return [
        remain * remain * remain / 6.0,
        (3.0 * cubed - 6.0 * square + 4.0) / 6.0,
        (-3.0 * cubed + 3.0 * square + 3.0 * frac + 1.0) / 6.0,
        cubed / 6.0,
    ]


def placed(gap, weights):
    out = jnp.zeros(gap.shape, F32)
    for j in range(4):
        out = jnp.where(gap == j, weights[j], out)
    return out


def squared_wave(group, inner, count):
    wave = jnp.where(inner < 2, 2 * group + inner, count - 2 * group - inner + 2)
    wave = jnp.where((inner == 2) & (group == 0), count // 2, wave)
    wave = jnp.where(wave < count // 2, wave, wave - count)
    return wave * wave


def hop_order(major, minor):
    def far(step, size):
        return min(step, size - step)

    steps = [(a, b) for a in range(major) for b in range(minor) if a or b]
    return sorted(steps, key=lambda s: (-far(s[0], major) - far(s[1], minor), abs(far(s[0], major) - far(s[1], minor)), s))


def kernel(
    groups, count_ref, charges_hbm, cot_hbm, base_hbm, frac_hbm, weights_hbm,
    za_hbm, xa_hbm, ya_hbm, yb_hbm, xb_hbm, zb_hbm,
    pot_ref, cg_ref, grad_ref,
    base_ref, frac_ref, both_ref, weights_ref, za_ref, xa_ref, ya_ref, yb_ref, xb_ref, zb_ref, load_sem,
    par_ref, near_par_ref, near_ref, wx_ref, wy_ref, wz_ref, st_ref, sn_ref, vals_ref, den_ref,
    s0_ref, r0_ref, s1_ref, r1_ref, s2_ref, r2_ref, s3_ref, r3_ref,
    wide_ref, line_ref, spec_ref, mirror_ref, prof_ref, shell_ref, corr_ref, field_ref, acc_ref, part_ref, back_ref,
    g1s_ref, g1r_ref, g2s_ref, g2r_ref, g3s_ref, g3r_ref,
    hs, hr, es, er, local_sem,
):
    G = groups
    N = 4 * G
    R = 4 * N
    si = lax.axis_index("slab")
    pi = lax.axis_index("pencil")
    where_is = {"slab": si, "pencil": pi}
    slots = charges_hbm.shape[1]

    barrier = pltpu.get_barrier_semaphore()

    def greet(d, carry):
        pl.semaphore_signal(barrier, inc=1, device_id={"pencil": lax.rem(pi + d, G)}, device_id_type=MESH)
        pl.semaphore_signal(barrier, inc=1, device_id={"slab": lax.rem(si + d, G)}, device_id_type=MESH)
        return carry

    lax.fori_loop(1, G, greet, 0)

    pairs = [
        (base_hbm, base_ref), (frac_hbm, frac_ref), (charges_hbm, both_ref.at[0:C]), (cot_hbm, both_ref.at[C:L]),
        (za_hbm, za_ref), (weights_hbm, weights_ref), (xa_hbm, xa_ref), (ya_hbm, ya_ref),
        (yb_hbm, yb_ref), (xb_hbm, xb_ref), (zb_hbm, zb_ref),
    ]
    owed = {}
    for i, (src, dst) in enumerate(pairs):
        load = pltpu.make_async_copy(src, dst, load_sem.at[i])
        load.start()
        owed["load", i] = load.wait

    def settle(*keys):
        for key in keys:
            owed.pop(key)()

    def shift(i, src, dst, step):
        copy = pltpu.make_async_remote_copy(
            src_ref=src, dst_ref=dst, send_sem=hs.at[i], recv_sem=hr.at[i],
            device_id={"pencil": lax.rem(pi + step + G, G)}, device_id_type=MESH,
        )
        copy.start()
        owed["shift", i] = copy.wait_recv
        owed["sent", i] = copy.wait_send

    def exchange(phase, src_of, dst, axis):
        me = where_is[axis]

        inner = 4 if axis == "slab" and G == 16 else 2
        for major, minor in hop_order(G // inner, inner):
            peer = lax.rem(lax.div(me, inner) + major, G // inner) * inner + lax.rem(lax.rem(me, inner) + minor, inner)
            pltpu.make_async_remote_copy(
                src_ref=src_of(peer), dst_ref=dst.at[me], send_sem=es.at[phase], recv_sem=er.at[phase],
                device_id={axis: peer}, device_id_type=MESH,
            ).start()
        others = dst.at[0:G - 1]
        owed["exchange", phase] = pltpu.make_async_copy(others, others, er.at[phase]).wait
        owed["gone", phase] = pltpu.make_async_copy(others, others, es.at[phase]).wait

    def begin(phase, src, dst, axis):
        me = where_is[axis]
        exchange(phase, lambda peer: src.at[peer], dst, axis)
        own = pltpu.make_async_copy(src.at[me], dst.at[me], local_sem.at[phase])
        own.start()
        owed["own", phase] = own.wait

    def finish(phase):
        settle(("exchange", phase), ("own", phase))

    lane = lax.broadcasted_iota(jnp.int32, (1, L), 1)
    sign = jnp.where(lane < C, 1.0, -1.0).astype(F32)

    def stage(table, pieces):
        columns = []
        for piece in pieces:
            wide = piece.astype(F32)
            turned = (pltpu.roll(wide, C, 1) * sign).astype(BF16)
            columns.append(jnp.concatenate([piece.astype(BF16), turned], axis=0))
        out = jnp.dot(table, jnp.concatenate(columns, axis=1), preferred_element_type=F32)
        return [out[:, i * L:(i + 1) * L] for i in range(len(pieces))]

    settle(("load", 0), ("load", 1))
    live = lax.broadcasted_iota(jnp.int32, (1, slots), 1) < count_ref[0]
    par_ref[0:3, :] = frac_ref[...]
    par_ref[3:6, :] = base_ref[...].astype(F32)
    par_ref[6:7, :] = live.astype(F32)
    par_ref[7:8, :] = jnp.zeros((1, slots), F32)
    settle(("load", 2), ("load", 3))
    pl.semaphore_wait(barrier, 2 * (G - 1))
    shift(0, par_ref, near_par_ref, 1)
    shift(1, both_ref, near_ref, 1)

    def weigh(par, block, first_row):
        row = lax.broadcasted_iota(jnp.int32, (8, slots), 0).astype(F32)
        wx = placed(row - (par[3:4, :] - (4 * si).astype(F32)), spline_weights(par[0:1, :]))
        wx_ref[...] = wx * par[6:7, :]
        wy_ref[...] = placed(row + first_row - (par[4:5, :] - (4 * block).astype(F32)), spline_weights(par[1:2, :]))
        gap = lax.broadcasted_iota(jnp.int32, (N, slots), 0).astype(F32) - par[5:6, :]
        wz_ref[...] = placed(jnp.where(gap < 0, gap + N, gap), spline_weights(par[2:3, :]))

    def spread(stencil_ref, x, rows):
        along_x = wx_ref[pl.ds(x, 1), :]
        for y in range(rows):
            stencil_ref[x, y] = (wz_ref[...] * (along_x * wy_ref[y:y + 1, :])).astype(BF16)
        left = stencil_ref[x].reshape(rows * N, slots)
        return jnp.dot(left, vals_ref[...], preferred_element_type=F32)

    def own_plane(x, carry):
        den_ref[x] = spread(st_ref, x, 4)
        return carry

    def near_plane(x, carry):
        den_ref[x, 0:3 * N] += spread(sn_ref, x, 3)
        return carry

    weigh(par_ref, pi, 0.0)
    vals_ref[...] = both_ref[...].T
    lax.fori_loop(0, 7, own_plane, 0)
    settle(("load", 4), ("shift", 0), ("shift", 1))
    weigh(near_par_ref, lax.rem(pi + G - 1, G), 4.0)
    vals_ref[...] = near_ref[...].T
    lax.fori_loop(0, 7, near_plane, 0)
    for x in range(0, 7, 2):
        pieces = [den_ref[i] for i in range(x, min(x + 2, 7))]
        for i, out in enumerate(stage(za_ref[...], pieces)):
            s0_ref[:, x + i] = out.astype(BF16).reshape(G, 16, L)
    begin(0, s0_ref, r0_ref, "slab")

    settle(*[("load", i) for i in range(5, 11)])
    at = lax.broadcasted_iota(jnp.int32, (NB, 16 * N), 1)
    along = at // 4 % N
    kappa_sq = (
        squared_wave(pi, at // R, N) + squared_wave(along // 4, along % 4, N) + squared_wave(si, at % 4, N)
    ).astype(F32)
    spacing = N / (2.0 * NB)
    centers = (lax.broadcasted_iota(jnp.int32, (NB, 16 * N), 0).astype(F32) + 0.5) * spacing
    reach = (jnp.sqrt(kappa_sq) - centers) / spacing
    shell_ref[...] = ENV_SCALE * ENV_WIDTH / (ENV_WIDTH + kappa_sq) * jnp.exp(-(reach * reach))
    doubled = jnp.concatenate([weights_ref[...], weights_ref[...]], axis=1)
    prof_ref[...] = lax.dot_general(
        shell_ref[...], doubled, (((0,), (0,)), ((), ())),
        precision=lax.Precision.HIGHEST, preferred_element_type=F32,
    ).reshape(4, R, L)

    finish(0)
    wide_ref[...] = r0_ref[...].reshape(7 * 16 * G, L).astype(F32)
    for b in range(0, 16, 2):
        outs = stage(xa_ref[...], [wide_ref[pl.ds(b + i, 7 * G, stride=16), :] for i in range(2)])
        for i in range(2):
            line_ref[pl.ds(b + i, N, stride=16), :] = outs[i]
    s1_ref[...] = line_ref[...].astype(BF16).reshape(G, 4, 16, L)
    begin(1, s1_ref, r1_ref, "pencil")
    finish(1)

    flip = jnp.where(si == 0, 1, 0)
    for x in range(0, 4, 2):
        outs = stage(ya_ref[flip], [r1_ref[:, x + i].reshape(R, L) for i in range(2)])
        for i in range(2):
            spec_ref[x + i] = outs[i][:R]
            mirror_ref[x + i] = outs[i][R:]
        outs = stage(yb_ref[...], [spec_ref[x + i] * prof_ref[x + i] for i in range(2)])
        for i in range(2):
            s2_ref[:, x + i] = outs[i].astype(BF16).reshape(G, 16, L)
    begin(2, s2_ref, r2_ref, "pencil")

    for x in range(4):
        opposite = jnp.where(pi == 0, (4 - x) % 4, (x + 2) % 4)
        corr_ref[pl.ds(x * R, R), :] = spec_ref[x] * pltpu.roll(mirror_ref[opposite], C, 1)
    partial = jnp.dot(
        shell_ref[...], corr_ref[...], precision=lax.Precision.HIGHEST, preferred_element_type=F32
    )
    partial = (partial + pltpu.roll(partial, C, 1)) * (0.5 / (N * N * N))
    rows = NB // G
    g1s_ref[...] = jnp.zeros_like(g1s_ref)
    for g in range(G):
        g1s_ref[g, 0:rows, :] = partial[g * rows:(g + 1) * rows]
    exchange(4, lambda peer: g1s_ref.at[peer], g1r_ref, "pencil")
    g1r_ref[pl.ds(pi, 1)] = g1s_ref[pl.ds(pi, 1)]

    finish(2)
    line_ref[...] = r2_ref[...].reshape(16 * N, L).astype(F32)
    for b in range(0, 16, 2):
        outs = stage(xb_ref[...], [line_ref[pl.ds(b + i, N, stride=16), :] for i in range(2)])
        for i in range(2):
            wide_ref[pl.ds(b + i, 7 * G, stride=16), :] = outs[i]
    s3_ref[...] = wide_ref[...].astype(BF16).reshape(G, 7, 16, L)
    begin(3, s3_ref, r3_ref, "slab")

    settle(("exchange", 4))
    total = jnp.sum(g1r_ref[...], axis=0)
    g2s_ref[...] = total
    exchange(5, lambda peer: g2s_ref, g2r_ref, "slab")
    g2r_ref[pl.ds(si, 1)] = total[None]

    finish(3)
    for x in range(0, 7, 2):
        pieces = [r3_ref[:, i].reshape(R, L) for i in range(x, min(x + 2, 7))]
        for i, out in enumerate(stage(zb_ref[...], pieces)):
            field_ref[x + i] = out.astype(BF16)

    def gathered(stencil_ref, rows):
        depth = 7 * rows * N
        return lax.dot_general(
            field_ref[:, 0:rows * N].reshape(depth, L), stencil_ref[...].reshape(depth, slots),
            (((0,), (0,)), ((), ())), preferred_element_type=F32,
        )

    part_ref[...] = gathered(sn_ref, 3).astype(BF16)
    shift(2, part_ref, back_ref, -1)

    settle(("exchange", 5))
    total = jnp.sum(g2r_ref[...], axis=0)
    g3s_ref[...] = total
    exchange(6, lambda peer: g3s_ref, g3r_ref, "pencil")
    g3r_ref[pl.ds(pi, 1)] = total[None]

    acc_ref[...] = gathered(st_ref, 4)
    settle(("shift", 2))
    pot_ref[...] = (acc_ref[0:C] + back_ref[0:C].astype(F32)).astype(BF16)
    cg_ref[...] = (acc_ref[C:L] + back_ref[C:L].astype(F32)).astype(BF16)

    settle(("exchange", 6))
    for g in range(G):
        grad_ref[g * rows:(g + 1) * rows, :] = g3r_ref[g, 0:rows, 0:C]
    for wait in owed.values():
        wait()


def per_device(charges, cotangent, base_cell, frac, counts, filter_weights):
    G = lax.axis_size("slab")
    N = 4 * G
    slots = charges.shape[1]
    dft = tables(G)
    vmem = pl.BlockSpec(memory_space=pltpu.VMEM)
    smem = pl.BlockSpec(memory_space=pltpu.SMEM)
    hbm = pl.BlockSpec(memory_space=pltpu.HBM)
    wide = pltpu.VMEM((G, 7, 16, L), BF16)
    slim = pltpu.VMEM((G, 4, 16, L), BF16)
    tiles = pltpu.VMEM((G, 8, L), F32)
    tile = pltpu.VMEM((8, L), F32)
    scratch = [
        pltpu.VMEM((3, slots), jnp.int32),
        pltpu.VMEM((3, slots), F32),
        pltpu.VMEM((L, slots), BF16),
        pltpu.VMEM((NB, C), F32),
        *[pltpu.VMEM(t.shape, BF16) for t in dft],
        pltpu.SemaphoreType.DMA((11,)),
        pltpu.VMEM((8, slots), F32),
        pltpu.VMEM((8, slots), F32),
        pltpu.VMEM((L, slots), BF16),
        pltpu.VMEM((8, slots), F32),
        pltpu.VMEM((8, slots), F32),
        pltpu.VMEM((N, slots), F32),
        pltpu.VMEM((7, 4, N, slots), BF16),
        pltpu.VMEM((7, 3, N, slots), BF16),
        pltpu.VMEM((slots, L), BF16),
        pltpu.VMEM((7, 4 * N, L), F32),
        wide, wide, slim, slim, slim, slim, wide, wide,
        pltpu.VMEM((7 * 16 * G, L), F32),
        pltpu.VMEM((16 * N, L), F32),
        pltpu.VMEM((4, 4 * N, L), F32),
        pltpu.VMEM((4, 4 * N, L), F32),
        pltpu.VMEM((4, 4 * N, L), F32),
        pltpu.VMEM((NB, 16 * N), F32),
        pltpu.VMEM((16 * N, L), F32),
        pltpu.VMEM((7, 4 * N, L), BF16),
        pltpu.VMEM((L, slots), F32),
        pltpu.VMEM((L, slots), BF16),
        pltpu.VMEM((L, slots), BF16),
        tiles, tiles, tile, tiles, tile, tiles,
        pltpu.SemaphoreType.DMA((3,)),
        pltpu.SemaphoreType.DMA((3,)),
        pltpu.SemaphoreType.DMA((7,)),
        pltpu.SemaphoreType.DMA((7,)),
        pltpu.SemaphoreType.DMA((4,)),
    ]
    return pl.pallas_call(
        functools.partial(kernel, G),
        out_shape=(
            jax.ShapeDtypeStruct((C, slots), BF16),
            jax.ShapeDtypeStruct((C, slots), BF16),
            jax.ShapeDtypeStruct((NB, C), F32),
        ),
        in_specs=[smem] + [hbm] * 11,
        out_specs=(vmem, vmem, vmem),
        scratch_shapes=scratch,
        compiler_params=pltpu.CompilerParams(
            collective_id=0, has_side_effects=True, vmem_limit_bytes=67043328
        ),
    )(counts, charges, cotangent, base_cell, frac, filter_weights, *dft)


def solution(mesh):
    spread = P(None, ("slab", "pencil"))
    return jax.shard_map(
        per_device,
        mesh=mesh,
        in_specs=(spread, spread, spread, spread, P(("slab", "pencil")), P()),
        out_specs=(spread, spread, P()),
        check_vma=False,
    )
```

```python
import functools

import jax
import jax.numpy as jnp
import numpy as np
from jax import lax
from jax.experimental import pallas as pl
from jax.experimental.pallas import tpu as pltpu
from jax.sharding import PartitionSpec as P

C = 64
L = 2 * C
NB = 32
ENV_SCALE = 40.0
ENV_WIDTH = 16.0
MESH = pl.DeviceIdType.MESH
F32 = jnp.float32
BF16 = jnp.bfloat16


def wave_order(groups):
    count = 4 * groups
    rows = []
    for g in range(groups):
        rows += [2 * g, 2 * g + 1, count - 2 * g if g else count // 2, count - 1 - 2 * g]
    return np.array(rows)


def tables(groups):
    count = 4 * groups
    waves = wave_order(groups)
    eye = np.eye(4)

    def parts(rows, cells, inverse):
        angles = (rows[:, None] * cells[None, :] % count) * (2.0 * np.pi / count)
        cosines, sines = np.cos(angles), np.sin(angles)
        return (cosines.T / count, -sines.T / count) if inverse else (cosines, sines)

    def joined(pair, pattern=None, inner=eye):
        size = 4 * count
        if pattern is not None:
            split = [t.reshape(groups, 4, groups, 4) for t in pair]
            pair = [np.einsum(pattern, t, inner).reshape(size, size) for t in split]
        return np.concatenate(pair, axis=1)

    every = np.arange(count)
    wide = (4 * np.arange(groups)[:, None] + np.arange(7)[None, :]).reshape(-1)
    ahead, back = parts(waves, every, False), parts(waves, every, True)
    mirror = parts((-waves) % count, every, False)
    y_ahead = joined(ahead, "glhm,ab->glahmb")
    across = [np.eye(4)[[(a + 2) % 4 for a in range(4)]], np.eye(4)[[(4 - a) % 4 for a in range(4)]]]
    halves = np.arange(4 * count).reshape(groups, 2, 2, 4).transpose(1, 0, 2, 3).reshape(-1)
    paired = np.concatenate([halves, halves + 4 * count])
    made = [
        joined(ahead, "glhm,yv->gylvhm")[halves],
        joined(parts(waves, wide, False)),
        y_ahead[:, paired],
        np.stack([joined(mirror, "glhm,ab->glahmb", t)[:, paired] for t in across]),
        joined(back, "glhm,ab->glahmb")[halves],
        joined(parts(waves, wide, True)),
        joined(back, "glhm,yv->yglhvm")[:, paired],
    ]
    return [jnp.asarray(t, BF16) for t in made]


def spline_weights(frac):
    remain = 1.0 - frac
    square = frac * frac
    cubed = square * frac
    return [
        remain * remain * remain / 6.0,
        (3.0 * cubed - 6.0 * square + 4.0) / 6.0,
        (-3.0 * cubed + 3.0 * square + 3.0 * frac + 1.0) / 6.0,
        cubed / 6.0,
    ]


def placed(gap, weights):
    out = jnp.zeros(gap.shape, F32)
    for j in range(4):
        out = jnp.where(gap == j, weights[j], out)
    return out


def squared_wave(group, inner, count):
    wave = jnp.where(inner < 2, 2 * group + inner, count - 2 * group - inner + 2)
    wave = jnp.where((inner == 2) & (group == 0), count // 2, wave)
    wave = jnp.where(wave < count // 2, wave, wave - count)
    return wave * wave


def hop_order(major, minor):
    def far(step, size):
        return min(step, size - step)

    steps = [(a, b) for a in range(major) for b in range(minor) if a or b]
    return sorted(steps, key=lambda s: (-far(s[0], major) - far(s[1], minor), abs(far(s[0], major) - far(s[1], minor)), s))


def kernel(
    groups, count_ref, charges_hbm, cot_hbm, base_hbm, frac_hbm, weights_hbm,
    za_hbm, xa_hbm, ya_hbm, ym_hbm, yb_hbm, xb_hbm, zb_hbm,
    pot_ref, cg_ref, grad_ref,
    base_ref, frac_ref, both_ref, weights_ref, za_ref, xa_ref, ya_ref, ym_ref, yb_ref, xb_ref, zb_ref, load_sem,
    live_ref, near_live_ref, near_frac_ref, near_base_ref, near_ref, wx_ref, wy_ref, wz_ref, st_ref, sn_ref, vals_ref, den_ref,
    s0_ref, r0_ref, s1_ref, r1_ref, s2_ref, r2_ref, s3_ref, r3_ref,
    wide_ref, line_ref, spec_ref, mirror_ref, prof_ref, shell_ref, corr_ref, field_ref, acc_ref, part_ref, back_ref,
    g1s_ref, g1r_ref, g2s_ref, g2r_ref, g3s_ref, g3r_ref,
    hs, hr, es, er, local_sem,
):
    G = groups
    N = 4 * G
    R = 4 * N
    si = lax.axis_index("slab")
    pi = lax.axis_index("pencil")
    where_is = {"slab": si, "pencil": pi}
    slots = charges_hbm.shape[1]

    barrier = pltpu.get_barrier_semaphore()

    def greet(d, carry):
        pl.semaphore_signal(barrier, inc=1, device_id={"pencil": lax.rem(pi + d, G)}, device_id_type=MESH)
        pl.semaphore_signal(barrier, inc=1, device_id={"slab": lax.rem(si + d, G)}, device_id_type=MESH)
        return carry

    lax.fori_loop(1, G, greet, 0)

    pairs = [
        (base_hbm, base_ref), (frac_hbm, frac_ref), (charges_hbm, both_ref.at[0:C]), (cot_hbm, both_ref.at[C:L]),
        (za_hbm, za_ref), (weights_hbm, weights_ref), (xa_hbm, xa_ref), (ya_hbm, ya_ref),
        (ym_hbm, ym_ref),
        (yb_hbm, yb_ref), (xb_hbm, xb_ref), (zb_hbm, zb_ref),
    ]
    owed = {}
    for i, (src, dst) in enumerate(pairs):
        load = pltpu.make_async_copy(src, dst, load_sem.at[i])
        load.start()
        owed["load", i] = load.wait

    def settle(*keys):
        for key in keys:
            owed.pop(key)()

    def shift(i, src, dst, step):
        copy = pltpu.make_async_remote_copy(
            src_ref=src, dst_ref=dst, send_sem=hs.at[i], recv_sem=hr.at[i],
            device_id={"pencil": lax.rem(pi + step + G, G)}, device_id_type=MESH,
        )
        copy.start()
        owed["shift", i] = copy.wait_recv
        owed["sent", i] = copy.wait_send

    def exchange(phase, src_of, dst, axis):
        me = where_is[axis]

        inner = 4 if axis == "slab" and G == 16 else 2
        for major, minor in hop_order(G // inner, inner):
            peer = lax.rem(lax.div(me, inner) + major, G // inner) * inner + lax.rem(lax.rem(me, inner) + minor, inner)
            pltpu.make_async_remote_copy(
                src_ref=src_of(peer), dst_ref=dst.at[me], send_sem=es.at[phase], recv_sem=er.at[phase],
                device_id={axis: peer}, device_id_type=MESH,
            ).start()
        others = dst.at[0:G - 1]
        owed["exchange", phase] = pltpu.make_async_copy(others, others, er.at[phase]).wait
        owed["gone", phase] = pltpu.make_async_copy(others, others, es.at[phase]).wait

    def begin(phase, src, dst, axis):
        me = where_is[axis]
        exchange(phase, lambda peer: src.at[peer], dst, axis)
        own = pltpu.make_async_copy(src.at[me], dst.at[me], local_sem.at[phase])
        own.start()
        owed["own", phase] = own.wait

    def finish(phase):
        settle(("exchange", phase), ("own", phase))

    lane = lax.broadcasted_iota(jnp.int32, (1, L), 1)
    sign = jnp.where(lane < C, 1.0, -1.0).astype(F32)

    def stage(table, pieces):
        columns = []
        for piece in pieces:
            wide = piece.astype(F32)
            turned = (pltpu.roll(wide, C, 1) * sign).astype(BF16)
            columns.append(jnp.concatenate([piece.astype(BF16), turned], axis=0))
        out = jnp.dot(table, jnp.concatenate(columns, axis=1), preferred_element_type=F32)
        return [out[:, i * L:(i + 1) * L] for i in range(len(pieces))]

    live = lax.broadcasted_iota(jnp.int32, (8, slots), 1) < count_ref[0]
    live_ref[...] = live.astype(F32)
    pl.semaphore_wait(barrier, 2 * (G - 1))
    shift(0, charges_hbm, near_ref.at[0:C], 1)
    shift(1, cot_hbm, near_ref.at[C:L], 1)
    shift(2, frac_hbm, near_frac_ref, 1)
    shift(3, base_hbm, near_base_ref, 1)
    shift(4, live_ref, near_live_ref, 1)

    def weigh(frac, base, alive, block, first_row):
        row = lax.broadcasted_iota(jnp.int32, (8, slots), 0)
        wx_ref[...] = placed(row - (base[0:1, :] - 4 * si), spline_weights(frac[0:1, :])) * alive[...]
        wy_ref[...] = placed(row + first_row - (base[1:2, :] - 4 * block), spline_weights(frac[1:2, :]))
        gap = lax.broadcasted_iota(jnp.int32, (N, slots), 0) - base[2:3, :]
        wz_ref[...] = placed(jnp.where(gap < 0, gap + N, gap), spline_weights(frac[2:3, :]))

    def spread(stencil_ref, x, rows):
        along_x = wx_ref[pl.ds(x, 1), :]
        for y in range(rows):
            stencil_ref[x, y] = (wz_ref[...] * (along_x * wy_ref[y:y + 1, :])).astype(BF16)
        left = stencil_ref[x].reshape(rows * N, slots)
        return jnp.dot(left, vals_ref[...], preferred_element_type=F32)

    def own_plane(x, carry):
        den_ref[x] = spread(st_ref, x, 4)
        return carry

    def near_plane(x, carry):
        den_ref[x, 0:3 * N] += spread(sn_ref, x, 3)
        return carry

    settle(("load", 0), ("load", 1))
    weigh(frac_ref, base_ref, live_ref, pi, 0)
    settle(("load", 2), ("load", 3))
    vals_ref[...] = both_ref[...].T
    lax.fori_loop(0, 7, own_plane, 0)
    settle(("load", 4), *[("shift", i) for i in range(5)])
    weigh(near_frac_ref, near_base_ref, near_live_ref, lax.rem(pi + G - 1, G), 4)
    vals_ref[...] = near_ref[...].T
    lax.fori_loop(0, 7, near_plane, 0)
    def in_halves(out):
        return [out[h * R // 2:(h + 1) * R // 2].astype(BF16).reshape(G, 8, L) for h in range(2)]

    def of_halves(ref, x):
        return jnp.concatenate([ref[h, :, x].reshape(R // 2, L) for h in range(2)], axis=0)

    for x in range(0, 7, 2):
        pieces = [den_ref[i] for i in range(x, min(x + 2, 7))]
        for i, out in enumerate(stage(za_ref[...], pieces)):
            for h, part in enumerate(in_halves(out)):
                s0_ref[h, :, x + i] = part
    for h in range(2):
        begin(h, s0_ref.at[h], r0_ref.at[h], "slab")

    settle(*[("load", i) for i in range(5, 12)])
    at = lax.broadcasted_iota(jnp.int32, (NB, 16 * N), 1)
    along = at // 4 % N
    kappa_sq = (
        squared_wave(pi, at // R, N) + squared_wave(along // 4, along % 4, N) + squared_wave(si, at % 4, N)
    ).astype(F32)
    spacing = N / (2.0 * NB)
    centers = (lax.broadcasted_iota(jnp.int32, (NB, 16 * N), 0).astype(F32) + 0.5) * spacing
    reach = (jnp.sqrt(kappa_sq) - centers) / spacing
    shell_ref[...] = ENV_SCALE * ENV_WIDTH / (ENV_WIDTH + kappa_sq) * jnp.exp(-(reach * reach))
    doubled = jnp.concatenate([weights_ref[...], weights_ref[...]], axis=1)
    prof_ref[...] = lax.dot_general(
        shell_ref[...], doubled, (((0,), (0,)), ((), ())),
        precision=lax.Precision.HIGHEST, preferred_element_type=F32,
    ).reshape(4, R, L)

    for h in range(2):
        finish(h)
        lo, hi = h * 56 * G, h * 8 * N
        wide_ref[lo:lo + 56 * G, :] = r0_ref[h].reshape(56 * G, L).astype(F32)
        for b in range(0, 8, 2):
            outs = stage(xa_ref[...], [wide_ref[pl.ds(lo + b + i, 7 * G, stride=8), :] for i in range(2)])
            for i in range(2):
                line_ref[pl.ds(hi + b + i, N, stride=8), :] = outs[i]
        s1_ref[h] = line_ref[hi:hi + 8 * N, :].astype(BF16).reshape(G, 4, 8, L)
        begin(2 + h, s1_ref.at[h], r1_ref.at[h], "pencil")
    finish(2)
    finish(3)

    for x in range(0, 4, 2):
        outs = stage(ya_ref[...], [of_halves(r1_ref, x + i) for i in range(2)])
        for i in range(2):
            spec_ref[x + i] = outs[i]
        outs = stage(yb_ref[...], [outs[i] * prof_ref[x + i] for i in range(2)])
        for i in range(2):
            for h, part in enumerate(in_halves(outs[i])):
                s2_ref[h, :, x + i] = part
    for h in range(2):
        begin(4 + h, s2_ref.at[h], r2_ref.at[h], "pencil")

    flip = jnp.where(si == 0, 1, 0)
    for x in range(0, 4, 2):
        outs = stage(ym_ref[flip], [of_halves(r1_ref, x + i) for i in range(2)])
        for i in range(2):
            mirror_ref[x + i] = outs[i]
    for x in range(4):
        opposite = jnp.where(pi == 0, (4 - x) % 4, (x + 2) % 4)
        corr_ref[pl.ds(x * R, R), :] = spec_ref[x] * pltpu.roll(mirror_ref[opposite], C, 1)
    partial = jnp.dot(
        shell_ref[...], corr_ref[...], precision=lax.Precision.HIGHEST, preferred_element_type=F32
    )
    partial = (partial + pltpu.roll(partial, C, 1)) * (0.5 / (N * N * N))
    rows = NB // G
    g1s_ref[...] = jnp.zeros_like(g1s_ref)
    for g in range(G):
        g1s_ref[g, 0:rows, :] = partial[g * rows:(g + 1) * rows]
    exchange(8, lambda peer: g1s_ref.at[peer], g1r_ref, "pencil")
    g1r_ref[pl.ds(pi, 1)] = g1s_ref[pl.ds(pi, 1)]

    for h in range(2):
        finish(4 + h)
        lo, hi = h * 56 * G, h * 8 * N
        line_ref[hi:hi + 8 * N, :] = r2_ref[h].reshape(8 * N, L).astype(F32)
        for b in range(0, 8, 2):
            outs = stage(xb_ref[...], [line_ref[pl.ds(hi + b + i, N, stride=8), :] for i in range(2)])
            for i in range(2):
                wide_ref[pl.ds(lo + b + i, 7 * G, stride=8), :] = outs[i]
        s3_ref[h] = wide_ref[lo:lo + 56 * G, :].astype(BF16).reshape(G, 7, 8, L)
        begin(6 + h, s3_ref.at[h], r3_ref.at[h], "slab")

    settle(("exchange", 8))
    total = jnp.sum(g1r_ref[...], axis=0)
    g2s_ref[...] = total
    exchange(9, lambda peer: g2s_ref, g2r_ref, "slab")
    g2r_ref[pl.ds(si, 1)] = total[None]

    finish(6)
    finish(7)
    for x in range(0, 7, 2):
        pieces = [of_halves(r3_ref, i) for i in range(x, min(x + 2, 7))]
        for i, out in enumerate(stage(zb_ref[...], pieces)):
            field_ref[x + i] = out.astype(BF16)

    def gathered(stencil_ref, rows):
        depth = 7 * rows * N
        return lax.dot_general(
            field_ref[:, 0:rows * N].reshape(depth, L), stencil_ref[...].reshape(depth, slots),
            (((0,), (0,)), ((), ())), preferred_element_type=F32,
        )

    part_ref[...] = gathered(sn_ref, 3).astype(BF16)
    shift(5, part_ref, back_ref, -1)

    settle(("exchange", 9))
    total = jnp.sum(g2r_ref[...], axis=0)
    g3s_ref[...] = total
    exchange(10, lambda peer: g3s_ref, g3r_ref, "pencil")
    g3r_ref[pl.ds(pi, 1)] = total[None]

    acc_ref[...] = gathered(st_ref, 4)
    settle(("shift", 5))
    pot_ref[...] = (acc_ref[0:C] + back_ref[0:C].astype(F32)).astype(BF16)
    cg_ref[...] = (acc_ref[C:L] + back_ref[C:L].astype(F32)).astype(BF16)

    settle(("exchange", 10))
    for g in range(G):
        grad_ref[g * rows:(g + 1) * rows, :] = g3r_ref[g, 0:rows, 0:C]
    for wait in owed.values():
        wait()


def deliver(pot_ref, cg_ref, grad_ref, pot_out, cg_out, grad_out, sems):
    pairs = [(pot_ref, pot_out), (cg_ref, cg_out), (grad_ref, grad_out)]
    copies = [pltpu.make_async_copy(src, dst, sems.at[i]) for i, (src, dst) in enumerate(pairs)]
    for copy in copies:
        copy.start()
    for copy in copies:
        copy.wait()


def per_device(charges, cotangent, base_cell, frac, counts, filter_weights):
    G = lax.axis_size("slab")
    N = 4 * G
    slots = charges.shape[1]
    dft = tables(G)
    vmem = pl.BlockSpec(memory_space=pltpu.VMEM)
    smem = pl.BlockSpec(memory_space=pltpu.SMEM)
    hbm = pl.BlockSpec(memory_space=pltpu.HBM)
    wide = pltpu.VMEM((2, G, 7, 8, L), BF16)
    slim = pltpu.VMEM((2, G, 4, 8, L), BF16)
    tiles = pltpu.VMEM((G, 8, L), F32)
    tile = pltpu.VMEM((8, L), F32)
    scratch = [
        pltpu.VMEM((3, slots), jnp.int32),
        pltpu.VMEM((3, slots), F32),
        pltpu.VMEM((L, slots), BF16),
        pltpu.VMEM((NB, C), F32),
        *[pltpu.VMEM(t.shape, BF16) for t in dft],
        pltpu.SemaphoreType.DMA((12,)),
        pltpu.VMEM((8, slots), F32),
        pltpu.VMEM((8, slots), F32),
        pltpu.VMEM((3, slots), F32),
        pltpu.VMEM((3, slots), jnp.int32),
        pltpu.VMEM((L, slots), BF16),
        pltpu.VMEM((8, slots), F32),
        pltpu.VMEM((8, slots), F32),
        pltpu.VMEM((N, slots), F32),
        pltpu.VMEM((7, 4, N, slots), BF16),
        pltpu.VMEM((7, 3, N, slots), BF16),
        pltpu.VMEM((slots, L), BF16),
        pltpu.VMEM((7, 4 * N, L), F32),
        wide, wide, slim, slim, slim, slim, wide, wide,
        pltpu.VMEM((7 * 16 * G, L), F32),
        pltpu.VMEM((16 * N, L), F32),
        pltpu.VMEM((4, 4 * N, L), F32),
        pltpu.VMEM((4, 4 * N, L), F32),
        pltpu.VMEM((4, 4 * N, L), F32),
        pltpu.VMEM((NB, 16 * N), F32),
        pltpu.VMEM((16 * N, L), F32),
        pltpu.VMEM((7, 4 * N, L), BF16),
        pltpu.VMEM((L, slots), F32),
        pltpu.VMEM((L, slots), BF16),
        pltpu.VMEM((L, slots), BF16),
        tiles, tiles, tile, tiles, tile, tiles,
        pltpu.SemaphoreType.DMA((6,)),
        pltpu.SemaphoreType.DMA((6,)),
        pltpu.SemaphoreType.DMA((11,)),
        pltpu.SemaphoreType.DMA((11,)),
        pltpu.SemaphoreType.DMA((8,)),
    ]
    shapes = (
        jax.ShapeDtypeStruct((C, slots), BF16),
        jax.ShapeDtypeStruct((C, slots), BF16),
        jax.ShapeDtypeStruct((NB, C), F32),
    )
    results = pl.pallas_call(
        functools.partial(kernel, G),
        out_shape=shapes,
        in_specs=[smem] + [hbm] * 12,
        out_specs=(vmem, vmem, vmem),
        scratch_shapes=scratch,
        compiler_params=pltpu.CompilerParams(
            collective_id=0, has_side_effects=True, vmem_limit_bytes=67043328
        ),
    )(counts, charges, cotangent, base_cell, frac, filter_weights, *dft)
    return pl.pallas_call(
        deliver,
        out_shape=shapes,
        in_specs=[hbm] * 3,
        out_specs=(vmem, vmem, vmem),
        scratch_shapes=[pltpu.SemaphoreType.DMA((3,))],
        compiler_params=pltpu.CompilerParams(vmem_limit_bytes=67043328),
    )(*results)


def solution(mesh):
    spread = P(None, ("slab", "pencil"))
    return jax.shard_map(
        per_device,
        mesh=mesh,
        in_specs=(spread, spread, spread, spread, P(("slab", "pencil")), P()),
        out_specs=(spread, spread, P()),
        check_vma=False,
    )
```

```python
import functools

import jax
import jax.numpy as jnp
import numpy as np
from jax import lax
from jax.experimental import pallas as pl
from jax.experimental.pallas import tpu as pltpu
from jax.sharding import PartitionSpec as P

C = 64
L = 2 * C
NB = 32
ENV_SCALE = 40.0
ENV_WIDTH = 16.0
MESH = pl.DeviceIdType.MESH
F32 = jnp.float32
BF16 = jnp.bfloat16


def wave_order(groups):
    count = 4 * groups
    rows = []
    for g in range(groups):
        rows += [2 * g, 2 * g + 1, count - 2 * g if g else count // 2, count - 1 - 2 * g]
    return np.array(rows)


def tables(groups):
    count = 4 * groups
    waves = wave_order(groups)
    eye = np.eye(4)

    def parts(rows, cells, inverse):
        angles = (rows[:, None] * cells[None, :] % count) * (2.0 * np.pi / count)
        cosines, sines = np.cos(angles), np.sin(angles)
        return (cosines.T / count, -sines.T / count) if inverse else (cosines, sines)

    def joined(pair, pattern=None, inner=eye):
        size = inner.shape[0] * count
        if pattern is not None:
            split = [t.reshape(groups, 4, groups, 4) for t in pair]
            pair = [np.einsum(pattern, t, inner).reshape(size, size) for t in split]
        return np.concatenate(pair, axis=1)

    every = np.arange(count)
    wide = (4 * np.arange(groups)[:, None] + np.arange(7)[None, :]).reshape(-1)
    ahead, back = parts(waves, every, False), parts(waves, every, True)
    mirror = parts((-waves) % count, every, False)
    y_ahead = joined(ahead, "glhm,ab->glahmb")
    across = [np.eye(4)[[(a + 2) % 4 for a in range(4)]], np.eye(4)[[(4 - a) % 4 for a in range(4)]]]
    halves = np.arange(4 * count).reshape(groups, 2, 2, 4).transpose(1, 0, 2, 3).reshape(-1)
    paired = np.concatenate([halves, halves + 4 * count])
    made = [
        joined(ahead, "glhm,yv->gylvhm", np.eye(2)),
        joined(parts(waves, wide, False)),
        y_ahead[:, paired],
        np.stack([joined(mirror, "glhm,ab->glahmb", t)[:, paired] for t in across]),
        joined(back, "glhm,ab->glahmb")[halves],
        joined(parts(waves, wide, True)),
        joined(back, "glhm,yv->yglhvm", np.eye(2)),
    ]
    return [jnp.asarray(t, BF16) for t in made]


def spline_weights(frac):
    remain = 1.0 - frac
    square = frac * frac
    cubed = square * frac
    return [
        remain * remain * remain / 6.0,
        (3.0 * cubed - 6.0 * square + 4.0) / 6.0,
        (-3.0 * cubed + 3.0 * square + 3.0 * frac + 1.0) / 6.0,
        cubed / 6.0,
    ]


def placed(gap, weights):
    out = jnp.zeros(gap.shape, F32)
    for j in range(4):
        out = jnp.where(gap == j, weights[j], out)
    return out


def squared_wave(group, inner, count):
    wave = jnp.where(inner < 2, 2 * group + inner, count - 2 * group - inner + 2)
    wave = jnp.where((inner == 2) & (group == 0), count // 2, wave)
    wave = jnp.where(wave < count // 2, wave, wave - count)
    return wave * wave


def hop_order(major, minor):
    def far(step, size):
        return min(step, size - step)

    steps = [(a, b) for a in range(major) for b in range(minor) if a or b]
    return sorted(steps, key=lambda s: (-far(s[0], major) - far(s[1], minor), abs(far(s[0], major) - far(s[1], minor)), s))


def kernel(
    groups, count_ref, charges_hbm, cot_hbm, base_hbm, frac_hbm, weights_hbm,
    za_hbm, xa_hbm, ya_hbm, ym_hbm, yb_hbm, xb_hbm, zb_hbm,
    pot_ref, cg_ref, grad_ref,
    base_ref, frac_ref, both_ref, weights_ref, za_ref, xa_ref, ya_ref, ym_ref, yb_ref, xb_ref, zb_ref, load_sem,
    live_ref, near_live_ref, near_frac_ref, near_base_ref, near_ref, wx_ref, wy_ref, wz_ref, st_ref, sn_ref, vals_ref, den_ref,
    s0_ref, r0_ref, s1_ref, r1_ref, s2_ref, r2_ref, s3_ref, r3_ref,
    wide_ref, line_ref, spec_ref, mirror_ref, prof_ref, shell_ref, corr_ref, field_ref, acc_ref, near_acc_ref, part_ref, back_ref,
    g1s_ref, g1r_ref, g2s_ref, g2r_ref, g3s_ref, g3r_ref,
    hs, hr, es, er, local_sem,
):
    G = groups
    N = 4 * G
    R = 4 * N
    si = lax.axis_index("slab")
    pi = lax.axis_index("pencil")
    where_is = {"slab": si, "pencil": pi}
    slots = charges_hbm.shape[1]

    barrier = pltpu.get_barrier_semaphore()

    def greet(d, carry):
        pl.semaphore_signal(barrier, inc=1, device_id={"pencil": lax.rem(pi + d, G)}, device_id_type=MESH)
        pl.semaphore_signal(barrier, inc=1, device_id={"slab": lax.rem(si + d, G)}, device_id_type=MESH)
        return carry

    lax.fori_loop(1, G, greet, 0)

    pairs = [
        (base_hbm, base_ref), (frac_hbm, frac_ref), (charges_hbm, both_ref.at[0:C]), (cot_hbm, both_ref.at[C:L]),
        (za_hbm, za_ref), (weights_hbm, weights_ref), (xa_hbm, xa_ref), (ya_hbm, ya_ref),
        (ym_hbm, ym_ref),
        (yb_hbm, yb_ref), (xb_hbm, xb_ref), (zb_hbm, zb_ref),
    ]
    owed = {}
    for i, (src, dst) in enumerate(pairs):
        load = pltpu.make_async_copy(src, dst, load_sem.at[i])
        load.start()
        owed["load", i] = load.wait

    def settle(*keys):
        for key in keys:
            owed.pop(key)()

    def shift(i, src, dst, step):
        copy = pltpu.make_async_remote_copy(
            src_ref=src, dst_ref=dst, send_sem=hs.at[i], recv_sem=hr.at[i],
            device_id={"pencil": lax.rem(pi + step + G, G)}, device_id_type=MESH,
        )
        copy.start()
        owed["shift", i] = copy.wait_recv
        owed["sent", i] = copy.wait_send

    def exchange(phase, src_of, dst, axis):
        me = where_is[axis]

        inner = 4 if axis == "slab" and G == 16 else 2
        for major, minor in hop_order(G // inner, inner):
            peer = lax.rem(lax.div(me, inner) + major, G // inner) * inner + lax.rem(lax.rem(me, inner) + minor, inner)
            pltpu.make_async_remote_copy(
                src_ref=src_of(peer), dst_ref=dst.at[me], send_sem=es.at[phase], recv_sem=er.at[phase],
                device_id={axis: peer}, device_id_type=MESH,
            ).start()
        others = dst.at[0:G - 1]
        owed["exchange", phase] = pltpu.make_async_copy(others, others, er.at[phase]).wait
        owed["gone", phase] = pltpu.make_async_copy(others, others, es.at[phase]).wait

    def begin(phase, src, dst, axis):
        me = where_is[axis]
        exchange(phase, lambda peer: src.at[peer], dst, axis)
        own = pltpu.make_async_copy(src.at[me], dst.at[me], local_sem.at[phase])
        own.start()
        owed["own", phase] = own.wait

    def finish(phase):
        settle(("exchange", phase), ("own", phase))

    lane = lax.broadcasted_iota(jnp.int32, (1, L), 1)
    sign = jnp.where(lane < C, 1.0, -1.0).astype(F32)

    def stage(table, pieces):
        columns = []
        for piece in pieces:
            wide = piece.astype(F32)
            turned = (pltpu.roll(wide, C, 1) * sign).astype(BF16)
            columns.append(jnp.concatenate([piece.astype(BF16), turned], axis=0))
        out = jnp.dot(table, jnp.concatenate(columns, axis=1), preferred_element_type=F32)
        return [out[:, i * L:(i + 1) * L] for i in range(len(pieces))]

    live = lax.broadcasted_iota(jnp.int32, (8, slots), 1) < count_ref[0]
    live_ref[...] = live.astype(F32)
    pl.semaphore_wait(barrier, 2 * (G - 1))
    shift(0, charges_hbm, near_ref.at[0:C], 1)
    shift(1, cot_hbm, near_ref.at[C:L], 1)
    shift(2, frac_hbm, near_frac_ref, 1)
    shift(3, base_hbm, near_base_ref, 1)
    shift(4, live_ref, near_live_ref, 1)

    def weigh(frac, base, alive, block, first_row):
        row = lax.broadcasted_iota(jnp.int32, (8, slots), 0)
        wx_ref[...] = placed(row - (base[0:1, :] - 4 * si), spline_weights(frac[0:1, :])) * alive[...]
        wy_ref[...] = placed(row + first_row - (base[1:2, :] - 4 * block), spline_weights(frac[1:2, :]))
        gap = lax.broadcasted_iota(jnp.int32, (N, slots), 0) - base[2:3, :]
        wz_ref[...] = placed(jnp.where(gap < 0, gap + N, gap), spline_weights(frac[2:3, :]))

    def spread(stencil_ref, x, first, last):
        along_x = wx_ref[pl.ds(x, 1), :]
        for y in range(first, last):
            stencil_ref[x, y] = (wz_ref[...] * (along_x * wy_ref[y:y + 1, :])).astype(BF16)
        left = stencil_ref[x, first:last].reshape((last - first) * N, slots)
        return jnp.dot(left, vals_ref[...], preferred_element_type=F32)

    def own_plane(x, carry):
        den_ref[x] = spread(st_ref, x, 0, 4)
        return carry

    def near_plane(first, last):
        def add(x, carry):
            den_ref[x, first * N:last * N] += spread(sn_ref, x, first, last)
            return carry

        return add

    settle(("load", 0), ("load", 1))
    weigh(frac_ref, base_ref, live_ref, pi, 0)
    settle(("load", 2), ("load", 3))
    vals_ref[...] = both_ref[...].T
    lax.fori_loop(0, 7, own_plane, 0)
    settle(("load", 4), *[("shift", i) for i in range(5)])
    weigh(near_frac_ref, near_base_ref, near_live_ref, lax.rem(pi + G - 1, G), 4)
    vals_ref[...] = near_ref[...].T
    def in_halves(out):
        return [out[h * R // 2:(h + 1) * R // 2].astype(BF16).reshape(G, 8, L) for h in range(2)]

    def of_halves(ref, x):
        return jnp.concatenate([ref[h, :, x].reshape(R // 2, L) for h in range(2)], axis=0)

    for h in range(2):
        lax.fori_loop(0, 7, near_plane(2 * h, min(2 * h + 2, 3)), 0)
        for x in range(0, 7, 2):
            pieces = [den_ref[i, h * R // 2:(h + 1) * R // 2] for i in range(x, min(x + 2, 7))]
            for i, out in enumerate(stage(za_ref[...], pieces)):
                s0_ref[h, :, x + i] = out.astype(BF16).reshape(G, 8, L)
        begin(h, s0_ref.at[h], r0_ref.at[h], "slab")

    settle(*[("load", i) for i in range(5, 12)])
    at = lax.broadcasted_iota(jnp.int32, (NB, 16 * N), 1)
    along = at // 4 % N
    kappa_sq = (
        squared_wave(pi, at // R, N) + squared_wave(along // 4, along % 4, N) + squared_wave(si, at % 4, N)
    ).astype(F32)
    spacing = N / (2.0 * NB)
    centers = (lax.broadcasted_iota(jnp.int32, (NB, 16 * N), 0).astype(F32) + 0.5) * spacing
    reach = (jnp.sqrt(kappa_sq) - centers) / spacing
    shell_ref[...] = ENV_SCALE * ENV_WIDTH / (ENV_WIDTH + kappa_sq) * jnp.exp(-(reach * reach))
    doubled = jnp.concatenate([weights_ref[...], weights_ref[...]], axis=1)
    prof_ref[...] = lax.dot_general(
        shell_ref[...], doubled, (((0,), (0,)), ((), ())),
        precision=lax.Precision.HIGHEST, preferred_element_type=F32,
    ).reshape(4, R, L)

    for h in range(2):
        finish(h)
        lo, hi = h * 56 * G, h * 8 * N
        wide_ref[lo:lo + 56 * G, :] = r0_ref[h].reshape(56 * G, L).astype(F32)
        for b in range(0, 8, 2):
            outs = stage(xa_ref[...], [wide_ref[pl.ds(lo + b + i, 7 * G, stride=8), :] for i in range(2)])
            for i in range(2):
                line_ref[pl.ds(hi + b + i, N, stride=8), :] = outs[i]
        s1_ref[h] = line_ref[hi:hi + 8 * N, :].astype(BF16).reshape(G, 4, 8, L)
        begin(2 + h, s1_ref.at[h], r1_ref.at[h], "pencil")
    finish(2)
    finish(3)

    for x in range(0, 4, 2):
        outs = stage(ya_ref[...], [of_halves(r1_ref, x + i) for i in range(2)])
        for i in range(2):
            spec_ref[x + i] = outs[i]
        outs = stage(yb_ref[...], [outs[i] * prof_ref[x + i] for i in range(2)])
        for i in range(2):
            for h, part in enumerate(in_halves(outs[i])):
                s2_ref[h, :, x + i] = part
    for h in range(2):
        begin(4 + h, s2_ref.at[h], r2_ref.at[h], "pencil")

    flip = jnp.where(si == 0, 1, 0)
    for x in range(0, 4, 2):
        outs = stage(ym_ref[flip], [of_halves(r1_ref, x + i) for i in range(2)])
        for i in range(2):
            mirror_ref[x + i] = outs[i]
    for x in range(4):
        opposite = jnp.where(pi == 0, (4 - x) % 4, (x + 2) % 4)
        corr_ref[pl.ds(x * R, R), :] = spec_ref[x] * pltpu.roll(mirror_ref[opposite], C, 1)
    partial = jnp.dot(
        shell_ref[...], corr_ref[...], precision=lax.Precision.HIGHEST, preferred_element_type=F32
    )
    partial = (partial + pltpu.roll(partial, C, 1)) * (0.5 / (N * N * N))
    rows = NB // G
    for g in range(G):
        g1s_ref[g] = partial[g * rows:(g + 1) * rows]
    exchange(8, lambda peer: g1s_ref.at[peer], g1r_ref, "pencil")
    g1r_ref[pl.ds(pi, 1)] = g1s_ref[pl.ds(pi, 1)]

    for h in range(2):
        finish(4 + h)
        lo, hi = h * 56 * G, h * 8 * N
        line_ref[hi:hi + 8 * N, :] = r2_ref[h].reshape(8 * N, L).astype(F32)
        for b in range(0, 8, 2):
            outs = stage(xb_ref[...], [line_ref[pl.ds(hi + b + i, N, stride=8), :] for i in range(2)])
            for i in range(2):
                wide_ref[pl.ds(lo + b + i, 7 * G, stride=8), :] = outs[i]
        s3_ref[h] = wide_ref[lo:lo + 56 * G, :].astype(BF16).reshape(G, 7, 8, L)
        begin(6 + h, s3_ref.at[h], r3_ref.at[h], "slab")

    settle(("exchange", 8))
    total = jnp.sum(g1r_ref[...], axis=0)
    g2s_ref[...] = total
    exchange(9, lambda peer: g2s_ref, g2r_ref, "slab")
    g2r_ref[pl.ds(si, 1)] = total[None]

    def gathered(stencil_ref, first, last):
        depth = 7 * (last - first) * N
        return lax.dot_general(
            field_ref[:, first * N:last * N].reshape(depth, L), stencil_ref[:, first:last].reshape(depth, slots),
            (((0,), (0,)), ((), ())), preferred_element_type=F32,
        )

    def field_half(h):
        for x in range(0, 7, 2):
            pieces = [r3_ref[h, :, i].reshape(R // 2, L) for i in range(x, min(x + 2, 7))]
            for i, out in enumerate(stage(zb_ref[...], pieces)):
                field_ref[x + i, h * R // 2:(h + 1) * R // 2] = out.astype(BF16)

    finish(6)
    field_half(0)
    near_acc_ref[...] = gathered(sn_ref, 0, 2)
    acc_ref[...] = gathered(st_ref, 0, 2)
    finish(7)
    field_half(1)
    part_ref[...] = (near_acc_ref[...] + gathered(sn_ref, 2, 3)).astype(BF16)
    shift(5, part_ref, back_ref, -1)

    settle(("exchange", 9))
    total = jnp.sum(g2r_ref[...], axis=0)
    g3s_ref[...] = total
    exchange(10, lambda peer: g3s_ref, g3r_ref, "pencil")
    g3r_ref[pl.ds(pi, 1)] = total[None]

    acc_ref[...] += gathered(st_ref, 2, 4)
    settle(("shift", 5))
    pot_ref[...] = (acc_ref[0:C] + back_ref[0:C].astype(F32)).astype(BF16)
    cg_ref[...] = (acc_ref[C:L] + back_ref[C:L].astype(F32)).astype(BF16)

    settle(("exchange", 10))
    for g in range(G):
        grad_ref[g * rows:(g + 1) * rows, :] = g3r_ref[g, :, 0:C]
    for wait in owed.values():
        wait()


def deliver(pot_ref, cg_ref, grad_ref, pot_out, cg_out, grad_out, sems):
    pairs = [(pot_ref, pot_out), (cg_ref, cg_out), (grad_ref, grad_out)]
    copies = [pltpu.make_async_copy(src, dst, sems.at[i]) for i, (src, dst) in enumerate(pairs)]
    for copy in copies:
        copy.start()
    for copy in copies:
        copy.wait()


def per_device(charges, cotangent, base_cell, frac, counts, filter_weights):
    G = lax.axis_size("slab")
    N = 4 * G
    slots = charges.shape[1]
    dft = tables(G)
    vmem = pl.BlockSpec(memory_space=pltpu.VMEM)
    smem = pl.BlockSpec(memory_space=pltpu.SMEM)
    hbm = pl.BlockSpec(memory_space=pltpu.HBM)
    wide = pltpu.VMEM((2, G, 7, 8, L), BF16)
    slim = pltpu.VMEM((2, G, 4, 8, L), BF16)
    tiles = pltpu.VMEM((G, NB // G, L), F32)
    tile = pltpu.VMEM((NB // G, L), F32)
    scratch = [
        pltpu.VMEM((3, slots), jnp.int32),
        pltpu.VMEM((3, slots), F32),
        pltpu.VMEM((L, slots), BF16),
        pltpu.VMEM((NB, C), F32),
        *[pltpu.VMEM(t.shape, BF16) for t in dft],
        pltpu.SemaphoreType.DMA((12,)),
        pltpu.VMEM((8, slots), F32),
        pltpu.VMEM((8, slots), F32),
        pltpu.VMEM((3, slots), F32),
        pltpu.VMEM((3, slots), jnp.int32),
        pltpu.VMEM((L, slots), BF16),
        pltpu.VMEM((8, slots), F32),
        pltpu.VMEM((8, slots), F32),
        pltpu.VMEM((N, slots), F32),
        pltpu.VMEM((7, 4, N, slots), BF16),
        pltpu.VMEM((7, 3, N, slots), BF16),
        pltpu.VMEM((slots, L), BF16),
        pltpu.VMEM((7, 4 * N, L), F32),
        wide, wide, slim, slim, slim, slim, wide, wide,
        pltpu.VMEM((7 * 16 * G, L), F32),
        pltpu.VMEM((16 * N, L), F32),
        pltpu.VMEM((4, 4 * N, L), F32),
        pltpu.VMEM((4, 4 * N, L), F32),
        pltpu.VMEM((4, 4 * N, L), F32),
        pltpu.VMEM((NB, 16 * N), F32),
        pltpu.VMEM((16 * N, L), F32),
        pltpu.VMEM((7, 4 * N, L), BF16),
        pltpu.VMEM((L, slots), F32),
        pltpu.VMEM((L, slots), F32),
        pltpu.VMEM((L, slots), BF16),
        pltpu.VMEM((L, slots), BF16),
        tiles, tiles, tile, tiles, tile, tiles,
        pltpu.SemaphoreType.DMA((6,)),
        pltpu.SemaphoreType.DMA((6,)),
        pltpu.SemaphoreType.DMA((11,)),
        pltpu.SemaphoreType.DMA((11,)),
        pltpu.SemaphoreType.DMA((8,)),
    ]
    shapes = (
        jax.ShapeDtypeStruct((C, slots), BF16),
        jax.ShapeDtypeStruct((C, slots), BF16),
        jax.ShapeDtypeStruct((NB, C), F32),
    )
    results = pl.pallas_call(
        functools.partial(kernel, G),
        out_shape=shapes,
        in_specs=[smem] + [hbm] * 12,
        out_specs=(vmem, vmem, vmem),
        scratch_shapes=scratch,
        compiler_params=pltpu.CompilerParams(
            collective_id=0, has_side_effects=True, vmem_limit_bytes=67043328
        ),
    )(counts, charges, cotangent, base_cell, frac, filter_weights, *dft)
    return pl.pallas_call(
        deliver,
        out_shape=shapes,
        in_specs=[hbm] * 3,
        out_specs=(vmem, vmem, vmem),
        scratch_shapes=[pltpu.SemaphoreType.DMA((3,))],
        compiler_params=pltpu.CompilerParams(vmem_limit_bytes=67043328),
    )(*results)


def solution(mesh):
    spread = P(None, ("slab", "pencil"))
    return jax.shard_map(
        per_device,
        mesh=mesh,
        in_specs=(spread, spread, spread, spread, P(("slab", "pencil")), P()),
        out_specs=(spread, spread, P()),
        check_vma=False,
    )
```

```python
import functools

import jax
import jax.numpy as jnp
import numpy as np
from jax import lax
from jax.experimental import pallas as pl
from jax.experimental.pallas import tpu as pltpu
from jax.sharding import PartitionSpec as P

C = 64
L = 2 * C
NB = 32
ENV_SCALE = 40.0
ENV_WIDTH = 16.0
MESH = pl.DeviceIdType.MESH
F32 = jnp.float32
BF16 = jnp.bfloat16


def wave_order(groups):
    count = 4 * groups
    rows = []
    for g in range(groups):
        rows += [2 * g, 2 * g + 1, count - 2 * g if g else count // 2, count - 1 - 2 * g]
    return np.array(rows)


def tables(groups):
    count = 4 * groups
    waves = wave_order(groups)
    eye = np.eye(4)

    def parts(rows, cells, inverse):
        angles = (rows[:, None] * cells[None, :] % count) * (2.0 * np.pi / count)
        cosines, sines = np.cos(angles), np.sin(angles)
        return (cosines.T / count, -sines.T / count) if inverse else (cosines, sines)

    def joined(pair, pattern=None, inner=eye):
        size = inner.shape[0] * count
        if pattern is not None:
            split = [t.reshape(groups, 4, groups, 4) for t in pair]
            pair = [np.einsum(pattern, t, inner).reshape(size, size) for t in split]
        return np.concatenate(pair, axis=1)

    every = np.arange(count)
    wide = (4 * np.arange(groups)[:, None] + np.arange(7)[None, :]).reshape(-1)
    ahead, back = parts(waves, every, False), parts(waves, every, True)
    mirror = parts((-waves) % count, every, False)
    y_ahead = joined(ahead, "glhm,ab->glahmb")
    across = [np.eye(4)[[(a + 2) % 4 for a in range(4)]], np.eye(4)[[(4 - a) % 4 for a in range(4)]]]
    halves = np.arange(4 * count).reshape(groups, 2, 2, 4).transpose(1, 0, 2, 3).reshape(-1)
    paired = np.concatenate([halves, halves + 4 * count])
    made = [
        joined(ahead, "glhm,yv->gylvhm", np.eye(2)),
        joined(parts(waves, wide, False)),
        y_ahead[:, paired],
        np.stack([joined(mirror, "glhm,ab->glahmb", t)[:, paired] for t in across]),
        joined(back, "glhm,ab->glahmb")[halves],
        joined(parts(waves, wide, True)),
        joined(back, "glhm,yv->yglhvm", np.eye(2)),
    ]
    return [jnp.asarray(t, BF16) for t in made]


def spline_weights(frac):
    remain = 1.0 - frac
    square = frac * frac
    cubed = square * frac
    return [
        remain * remain * remain / 6.0,
        (3.0 * cubed - 6.0 * square + 4.0) / 6.0,
        (-3.0 * cubed + 3.0 * square + 3.0 * frac + 1.0) / 6.0,
        cubed / 6.0,
    ]


def placed(gap, weights):
    out = jnp.zeros(gap.shape, F32)
    for j in range(4):
        out = jnp.where(gap == j, weights[j], out)
    return out


def squared_wave(group, inner, count):
    wave = jnp.where(inner < 2, 2 * group + inner, count - 2 * group - inner + 2)
    wave = jnp.where((inner == 2) & (group == 0), count // 2, wave)
    wave = jnp.where(wave < count // 2, wave, wave - count)
    return wave * wave


def hop_order(major, minor):
    def far(step, size):
        return min(step, size - step)

    steps = [(a, b) for a in range(major) for b in range(minor) if a or b]
    return sorted(steps, key=lambda s: (-far(s[0], major) - far(s[1], minor), abs(far(s[0], major) - far(s[1], minor)), s))


def kernel(
    groups, count_ref, charges_hbm, cot_hbm, base_hbm, frac_hbm, weights_hbm,
    za_hbm, xa_hbm, ya_hbm, ym_hbm, yb_hbm, xb_hbm, zb_hbm,
    pot_ref, cg_ref, grad_ref,
    base_ref, frac_ref, both_ref, weights_ref, za_ref, xa_ref, ya_ref, ym_ref, yb_ref, xb_ref, zb_ref, load_sem,
    live_ref, near_live_ref, near_frac_ref, near_base_ref, near_ref, wx_ref, wy_ref, wz_ref, st_ref, sn_ref, vals_ref, den_ref,
    s0_ref, r0_ref, s1_ref, r1_ref, s2_ref, r2_ref, s3_ref, r3_ref,
    wide_ref, line_ref, spec_ref, mirror_ref, prof_ref, shell_ref, corr_ref, field_ref, acc_ref, near_acc_ref, part_ref, back_ref,
    g1s_ref, g1r_ref, g2s_ref, g2r_ref, g3s_ref, g3r_ref,
    hs, hr, es, er, local_sem,
):
    G = groups
    N = 4 * G
    R = 4 * N
    si = lax.axis_index("slab")
    pi = lax.axis_index("pencil")
    where_is = {"slab": si, "pencil": pi}
    slots = charges_hbm.shape[1]

    barrier = pltpu.get_barrier_semaphore()

    def greet(d, carry):
        pl.semaphore_signal(barrier, inc=1, device_id={"pencil": lax.rem(pi + d, G)}, device_id_type=MESH)
        pl.semaphore_signal(barrier, inc=1, device_id={"slab": lax.rem(si + d, G)}, device_id_type=MESH)
        return carry

    lax.fori_loop(1, G, greet, 0)

    pairs = [
        (base_hbm, base_ref), (frac_hbm, frac_ref), (charges_hbm, both_ref.at[0:C]), (cot_hbm, both_ref.at[C:L]),
        (za_hbm, za_ref), (weights_hbm, weights_ref), (xa_hbm, xa_ref), (ya_hbm, ya_ref),
        (ym_hbm, ym_ref),
        (yb_hbm, yb_ref), (xb_hbm, xb_ref), (zb_hbm, zb_ref),
    ]
    owed = {}
    for i, (src, dst) in enumerate(pairs):
        load = pltpu.make_async_copy(src, dst, load_sem.at[i])
        load.start()
        owed["load", i] = load.wait

    def settle(*keys):
        for key in keys:
            owed.pop(key)()

    def shift(i, src, dst, step):
        copy = pltpu.make_async_remote_copy(
            src_ref=src, dst_ref=dst, send_sem=hs.at[i], recv_sem=hr.at[i],
            device_id={"pencil": lax.rem(pi + step + G, G)}, device_id_type=MESH,
        )
        copy.start()
        owed["shift", i] = copy.wait_recv
        owed["sent", i] = copy.wait_send

    def exchange(phase, src_of, dst, axis):
        me = where_is[axis]

        inner = 4 if axis == "slab" and G == 16 else 2
        for major, minor in hop_order(G // inner, inner):
            peer = lax.rem(lax.div(me, inner) + major, G // inner) * inner + lax.rem(lax.rem(me, inner) + minor, inner)
            pltpu.make_async_remote_copy(
                src_ref=src_of(peer), dst_ref=dst.at[me], send_sem=es.at[phase], recv_sem=er.at[phase],
                device_id={axis: peer}, device_id_type=MESH,
            ).start()
        others = dst.at[0:G - 1]
        owed["exchange", phase] = pltpu.make_async_copy(others, others, er.at[phase]).wait
        owed["gone", phase] = pltpu.make_async_copy(others, others, es.at[phase]).wait

    def begin(phase, src, dst, axis):
        me = where_is[axis]
        exchange(phase, lambda peer: src.at[peer], dst, axis)
        own = pltpu.make_async_copy(src.at[me], dst.at[me], local_sem.at[phase])
        own.start()
        owed["own", phase] = own.wait

    def finish(phase):
        settle(("exchange", phase), ("own", phase))

    lane = lax.broadcasted_iota(jnp.int32, (1, L), 1)
    sign = jnp.where(lane < C, 1.0, -1.0).astype(F32)

    def stage(table, pieces):
        columns = []
        for piece in pieces:
            wide = piece.astype(F32)
            turned = (pltpu.roll(wide, C, 1) * sign).astype(BF16)
            columns.append(jnp.concatenate([piece.astype(BF16), turned], axis=0))
        out = jnp.dot(table, jnp.concatenate(columns, axis=1), preferred_element_type=F32)
        return [out[:, i * L:(i + 1) * L] for i in range(len(pieces))]

    live = lax.broadcasted_iota(jnp.int32, (8, slots), 1) < count_ref[0]
    live_ref[...] = live.astype(F32)
    pl.semaphore_wait(barrier, 2 * (G - 1))
    shift(2, frac_hbm, near_frac_ref, 1)
    shift(3, base_hbm, near_base_ref, 1)
    shift(4, live_ref, near_live_ref, 1)
    shift(0, charges_hbm, near_ref.at[0:C], 1)
    shift(1, cot_hbm, near_ref.at[C:L], 1)

    def weigh(frac, base, alive, block, first_row):
        row = lax.broadcasted_iota(jnp.int32, (8, slots), 0)
        wx_ref[...] = placed(row - (base[0:1, :] - 4 * si), spline_weights(frac[0:1, :])) * alive[...]
        wy_ref[...] = placed(row + first_row - (base[1:2, :] - 4 * block), spline_weights(frac[1:2, :]))
        gap = lax.broadcasted_iota(jnp.int32, (N, slots), 0) - base[2:3, :]
        wz_ref[...] = placed(jnp.where(gap < 0, gap + N, gap), spline_weights(frac[2:3, :]))

    def stencil_plane(stencil_ref, x, rows):
        along_x = wx_ref[pl.ds(x, 1), :]
        for y in range(rows):
            stencil_ref[x, y] = (wz_ref[...] * (along_x * wy_ref[y:y + 1, :])).astype(BF16)

    def spread(stencil_ref, x, first, last):
        left = stencil_ref[x, first:last].reshape((last - first) * N, slots)
        return jnp.dot(left, vals_ref[...], preferred_element_type=F32)

    def own_plane(x, carry):
        stencil_plane(st_ref, x, 4)
        den_ref[x] = spread(st_ref, x, 0, 4)
        return carry

    def near_stencil(x, carry):
        stencil_plane(sn_ref, x, 3)
        return carry

    def near_plane(first, last):
        def add(x, carry):
            den_ref[x, first * N:last * N] += spread(sn_ref, x, first, last)
            return carry

        return add

    settle(("load", 0), ("load", 1))
    weigh(frac_ref, base_ref, live_ref, pi, 0)
    settle(("load", 2), ("load", 3))
    vals_ref[...] = both_ref[...].T
    lax.fori_loop(0, 7, own_plane, 0)
    settle(*[("shift", i) for i in range(2, 5)])
    weigh(near_frac_ref, near_base_ref, near_live_ref, lax.rem(pi + G - 1, G), 4)
    lax.fori_loop(0, 7, near_stencil, 0)
    settle(("load", 4), ("shift", 0), ("shift", 1))
    vals_ref[...] = near_ref[...].T
    def in_halves(out):
        return [out[h * R // 2:(h + 1) * R // 2].astype(BF16).reshape(G, 8, L) for h in range(2)]

    def of_halves(ref, x):
        return jnp.concatenate([ref[h, :, x].reshape(R // 2, L) for h in range(2)], axis=0)

    for h in range(2):
        lax.fori_loop(0, 7, near_plane(2 * h, min(2 * h + 2, 3)), 0, unroll=True)
        for x in range(0, 7, 2):
            pieces = [den_ref[i, h * R // 2:(h + 1) * R // 2] for i in range(x, min(x + 2, 7))]
            for i, out in enumerate(stage(za_ref[...], pieces)):
                s0_ref[h, :, x + i] = out.astype(BF16).reshape(G, 8, L)
        begin(h, s0_ref.at[h], r0_ref.at[h], "slab")

    settle(*[("load", i) for i in range(5, 12)])
    at = lax.broadcasted_iota(jnp.int32, (NB, 16 * N), 1)
    along = at // 4 % N
    kappa_sq = (
        squared_wave(pi, at // R, N) + squared_wave(along // 4, along % 4, N) + squared_wave(si, at % 4, N)
    ).astype(F32)
    spacing = N / (2.0 * NB)
    centers = (lax.broadcasted_iota(jnp.int32, (NB, 16 * N), 0).astype(F32) + 0.5) * spacing
    reach = (jnp.sqrt(kappa_sq) - centers) / spacing
    shell_ref[...] = ENV_SCALE * ENV_WIDTH / (ENV_WIDTH + kappa_sq) * jnp.exp(-(reach * reach))
    doubled = jnp.concatenate([weights_ref[...], weights_ref[...]], axis=1)
    prof_ref[...] = lax.dot_general(
        shell_ref[...], doubled, (((0,), (0,)), ((), ())),
        precision=lax.Precision.HIGHEST, preferred_element_type=F32,
    ).reshape(4, R, L)

    for h in range(2):
        finish(h)
        lo, hi = h * 56 * G, h * 8 * N
        wide_ref[lo:lo + 56 * G, :] = r0_ref[h].reshape(56 * G, L).astype(F32)
        for b in range(0, 8, 2):
            outs = stage(xa_ref[...], [wide_ref[pl.ds(lo + b + i, 7 * G, stride=8), :] for i in range(2)])
            for i in range(2):
                line_ref[pl.ds(hi + b + i, N, stride=8), :] = outs[i]
        s1_ref[h] = line_ref[hi:hi + 8 * N, :].astype(BF16).reshape(G, 4, 8, L)
        begin(2 + h, s1_ref.at[h], r1_ref.at[h], "pencil")
    finish(2)
    finish(3)

    for x in range(0, 4, 2):
        outs = stage(ya_ref[...], [of_halves(r1_ref, x + i) for i in range(2)])
        for i in range(2):
            spec_ref[x + i] = outs[i]
        outs = stage(yb_ref[...], [outs[i] * prof_ref[x + i] for i in range(2)])
        for i in range(2):
            for h, part in enumerate(in_halves(outs[i])):
                s2_ref[h, :, x + i] = part
    for h in range(2):
        begin(4 + h, s2_ref.at[h], r2_ref.at[h], "pencil")

    flip = jnp.where(si == 0, 1, 0)
    for x in range(0, 4, 2):
        outs = stage(ym_ref[flip], [of_halves(r1_ref, x + i) for i in range(2)])
        for i in range(2):
            mirror_ref[x + i] = outs[i]
    for x in range(4):
        opposite = jnp.where(pi == 0, (4 - x) % 4, (x + 2) % 4)
        corr_ref[pl.ds(x * R, R), :] = spec_ref[x] * pltpu.roll(mirror_ref[opposite], C, 1)
    partial = jnp.dot(
        shell_ref[...], corr_ref[...], precision=lax.Precision.HIGHEST, preferred_element_type=F32
    )
    partial = (partial + pltpu.roll(partial, C, 1)) * (0.5 / (N * N * N))
    rows = NB // G
    for g in range(G):
        g1s_ref[g] = partial[g * rows:(g + 1) * rows]
    exchange(8, lambda peer: g1s_ref.at[peer], g1r_ref, "pencil")
    g1r_ref[pl.ds(pi, 1)] = g1s_ref[pl.ds(pi, 1)]

    for h in range(2):
        finish(4 + h)
        lo, hi = h * 56 * G, h * 8 * N
        line_ref[hi:hi + 8 * N, :] = r2_ref[h].reshape(8 * N, L).astype(F32)
        for b in range(0, 8, 2):
            outs = stage(xb_ref[...], [line_ref[pl.ds(hi + b + i, N, stride=8), :] for i in range(2)])
            for i in range(2):
                wide_ref[pl.ds(lo + b + i, 7 * G, stride=8), :] = outs[i]
        s3_ref[h] = wide_ref[lo:lo + 56 * G, :].astype(BF16).reshape(G, 7, 8, L)
        begin(6 + h, s3_ref.at[h], r3_ref.at[h], "slab")

    settle(("exchange", 8))
    total = jnp.sum(g1r_ref[...], axis=0)
    g2s_ref[...] = total
    exchange(9, lambda peer: g2s_ref, g2r_ref, "slab")
    g2r_ref[pl.ds(si, 1)] = total[None]

    def gathered(stencil_ref, first, last):
        depth = 7 * (last - first) * N
        return lax.dot_general(
            field_ref[:, first * N:last * N].reshape(depth, L), stencil_ref[:, first:last].reshape(depth, slots),
            (((0,), (0,)), ((), ())), preferred_element_type=F32,
        )

    def field_half(h):
        for x in range(0, 7, 2):
            pieces = [r3_ref[h, :, i].reshape(R // 2, L) for i in range(x, min(x + 2, 7))]
            for i, out in enumerate(stage(zb_ref[...], pieces)):
                field_ref[x + i, h * R // 2:(h + 1) * R // 2] = out.astype(BF16)

    finish(6)
    field_half(0)
    near_acc_ref[...] = gathered(sn_ref, 0, 2)
    acc_ref[...] = gathered(st_ref, 0, 2)
    finish(7)
    field_half(1)
    part_ref[...] = (near_acc_ref[...] + gathered(sn_ref, 2, 3)).astype(BF16)
    shift(5, part_ref, back_ref, -1)

    settle(("exchange", 9))
    total = jnp.sum(g2r_ref[...], axis=0)
    g3s_ref[...] = total
    exchange(10, lambda peer: g3s_ref, g3r_ref, "pencil")
    g3r_ref[pl.ds(pi, 1)] = total[None]

    acc_ref[...] += gathered(st_ref, 2, 4)
    settle(("shift", 5))
    pot_ref[...] = (acc_ref[0:C] + back_ref[0:C].astype(F32)).astype(BF16)
    cg_ref[...] = (acc_ref[C:L] + back_ref[C:L].astype(F32)).astype(BF16)

    settle(("exchange", 10))
    for g in range(G):
        grad_ref[g * rows:(g + 1) * rows, :] = g3r_ref[g, :, 0:C]
    for wait in owed.values():
        wait()


def deliver(pot_ref, cg_ref, grad_ref, pot_out, cg_out, grad_out, sems):
    pairs = [(pot_ref, pot_out), (cg_ref, cg_out), (grad_ref, grad_out)]
    copies = [pltpu.make_async_copy(src, dst, sems.at[i]) for i, (src, dst) in enumerate(pairs)]
    for copy in copies:
        copy.start()
    for copy in copies:
        copy.wait()


def per_device(charges, cotangent, base_cell, frac, counts, filter_weights):
    G = lax.axis_size("slab")
    N = 4 * G
    slots = charges.shape[1]
    dft = tables(G)
    vmem = pl.BlockSpec(memory_space=pltpu.VMEM)
    smem = pl.BlockSpec(memory_space=pltpu.SMEM)
    hbm = pl.BlockSpec(memory_space=pltpu.HBM)
    wide = pltpu.VMEM((2, G, 7, 8, L), BF16)
    slim = pltpu.VMEM((2, G, 4, 8, L), BF16)
    tiles = pltpu.VMEM((G, NB // G, L), F32)
    tile = pltpu.VMEM((NB // G, L), F32)
    scratch = [
        pltpu.VMEM((3, slots), jnp.int32),
        pltpu.VMEM((3, slots), F32),
        pltpu.VMEM((L, slots), BF16),
        pltpu.VMEM((NB, C), F32),
        *[pltpu.VMEM(t.shape, BF16) for t in dft],
        pltpu.SemaphoreType.DMA((12,)),
        pltpu.VMEM((8, slots), F32),
        pltpu.VMEM((8, slots), F32),
        pltpu.VMEM((3, slots), F32),
        pltpu.VMEM((3, slots), jnp.int32),
        pltpu.VMEM((L, slots), BF16),
        pltpu.VMEM((8, slots), F32),
        pltpu.VMEM((8, slots), F32),
        pltpu.VMEM((N, slots), F32),
        pltpu.VMEM((7, 4, N, slots), BF16),
        pltpu.VMEM((7, 3, N, slots), BF16),
        pltpu.VMEM((slots, L), BF16),
        pltpu.VMEM((7, 4 * N, L), F32),
        wide, wide, slim, slim, slim, slim, wide, wide,
        pltpu.VMEM((7 * 16 * G, L), F32),
        pltpu.VMEM((16 * N, L), F32),
        pltpu.VMEM((4, 4 * N, L), F32),
        pltpu.VMEM((4, 4 * N, L), F32),
        pltpu.VMEM((4, 4 * N, L), F32),
        pltpu.VMEM((NB, 16 * N), F32),
        pltpu.VMEM((16 * N, L), F32),
        pltpu.VMEM((7, 4 * N, L), BF16),
        pltpu.VMEM((L, slots), F32),
        pltpu.VMEM((L, slots), F32),
        pltpu.VMEM((L, slots), BF16),
        pltpu.VMEM((L, slots), BF16),
        tiles, tiles, tile, tiles, tile, tiles,
        pltpu.SemaphoreType.DMA((6,)),
        pltpu.SemaphoreType.DMA((6,)),
        pltpu.SemaphoreType.DMA((11,)),
        pltpu.SemaphoreType.DMA((11,)),
        pltpu.SemaphoreType.DMA((8,)),
    ]
    shapes = (
        jax.ShapeDtypeStruct((C, slots), BF16),
        jax.ShapeDtypeStruct((C, slots), BF16),
        jax.ShapeDtypeStruct((NB, C), F32),
    )
    results = pl.pallas_call(
        functools.partial(kernel, G),
        out_shape=shapes,
        in_specs=[smem] + [hbm] * 12,
        out_specs=(vmem, vmem, vmem),
        scratch_shapes=scratch,
        compiler_params=pltpu.CompilerParams(
            collective_id=0, has_side_effects=True, vmem_limit_bytes=67043328
        ),
    )(counts, charges, cotangent, base_cell, frac, filter_weights, *dft)
    return pl.pallas_call(
        deliver,
        out_shape=shapes,
        in_specs=[hbm] * 3,
        out_specs=(vmem, vmem, vmem),
        scratch_shapes=[pltpu.SemaphoreType.DMA((3,))],
        compiler_params=pltpu.CompilerParams(vmem_limit_bytes=67043328),
    )(*results)


def solution(mesh):
    spread = P(None, ("slab", "pencil"))
    return jax.shard_map(
        per_device,
        mesh=mesh,
        in_specs=(spread, spread, spread, spread, P(("slab", "pencil")), P()),
        out_specs=(spread, spread, P()),
        check_vma=False,
    )
```
